256 devices in a mesh: ctx: 8 (over y, core), exp: 32 (over x, z).
Axes of the slice: x: 4, y: 4, z: 8, core: 2. Of those that a mesh axis runs over, the one named last changes fastest.
Arguments:
- hidden: bfloat16 [32, 1024, 2048], P('exp', 'ctx'), may hold values from -6 to 6
- queries: bfloat16 [32, 1024, 1536], P('exp', 'ctx'), may hold values from -48 to 48
- latent: bfloat16 [32, 1024, 576], P('exp', 'ctx'), may hold values from -48 to 48
- group_order: int32 [16], replicated, may hold values from 0 to 15, each once
- w_uk: bfloat16 [512, 1024], replicated, may hold values from -0.25 to 0.25
- w_uv: bfloat16 [512, 1024], replicated, may hold values from -0.25 to 0.25
- w_out: bfloat16 [1024, 2048], replicated, may hold values from -0.1875 to 0.1875
- norm_gain: float32 [2048], replicated, may hold values from 0.5 to 1.5
- expert_ids: int32 [32, 1024, 6], P('exp', 'ctx'), may hold values from 0 to 63, all different within a row; in each aligned block of 128 rows (0 to 127, 128 to 255, ..., all dimensions but the last counted through in order) at most 13 rows name the same one
- gate_weights: float32 [32, 1024, 6], P('exp', 'ctx'), may hold values from 0.05 to 0.5
- w_gate: bfloat16 [64, 2048, 1024], P('exp', None, 'ctx'), may hold values from -0.125 to 0.125
- w_up: bfloat16 [64, 2048, 1024], P('exp', None, 'ctx'), may hold values from -0.125 to 0.125
- w_down: bfloat16 [64, 2048, 1024], P('exp', None, 'ctx'), may hold values from -0.1875 to 0.1875
Outputs:
- mixed: bfloat16 [32, 1024, 2048], P('exp', 'ctx')
The draws below stay inside these ranges and needn't reach their ends.
Inputs may be any that keep to these rules, and one draw needn't show every extreme that they name: `expert_ids`: within each aligned block of 128 rows of a sequence (the rows of one device), each expert is named by at most 13 rows, a bound that some block reaches; each row names 6 different experts. A permutation; stored half-block i of 64 rows holds the positions of half-block group_order[i], in increasing order.
All inputs are finite; a program needn't handle non-finite values.
Results may differ from the reference program's by a relative error of at most 0.011.
Values may be sent and summed in bfloat16 or wider, within the bound.
No kernel may reach another device: no remote copies, remote signals or barrier semaphores. Data moves between devices by JAX's collectives and lax.ppermute only.
A program may use at most 192 MiB of HBM per device.

```python
import math
import jax
import jax.numpy as jnp
import numpy as np
from jax import lax

D = 2048
HEADS = 8
NOPE = 128
ROPE = 64
VDIM = 128
KVR = 512
MOE_FF = 1024
EXPERTS = 64
TOPK = 6
TOK_DEV = 128
HALF = 64
SEQ = 1024
BATCH = 32
CAP = 13
N_CTX = 8


def joint_draw(key):
    query_key = jax.random.fold_in(key, 101)
    latent_key = jax.random.fold_in(key, 202)
    query_all = jnp.clip(jax.random.normal(query_key, (BATCH, SEQ, HEADS, NOPE + ROPE), jnp.float32), -5.0, 5.0)
    latent_all = jnp.clip(jax.random.normal(latent_key, (BATCH, SEQ, KVR + ROPE), jnp.float32), -5.0, 5.0)
    return (query_all.reshape(BATCH, SEQ, HEADS * (NOPE + ROPE)), latent_all)


def draw_queries(key, part):
    return joint_draw(key)[0].astype(jnp.bfloat16)


def draw_latent(key, part):
    return joint_draw(key)[1].astype(jnp.bfloat16)


def block_scale(stream_key, shape, split, least, high):
    factor_of, own = 1.0, jax.random.fold_in(stream_key, 6)
    for axis_at, parts in split:
        steps = jnp.exp(jax.random.uniform(jax.random.fold_in(own, axis_at), (parts,), jnp.float32, least / len(split), high / len(split)))
        factor_of = factor_of * jnp.repeat(steps, shape[axis_at] // parts).reshape([-1 if axis == axis_at else 1 for axis in range(len(shape))])
    return factor_of


def assign_block(rng, own, number, rows, number_of, top, reach, slope):
    sequence = jax.random.permutation(rng, number_of)
    crowded, common = shares(number_of, rows * top, reach, slope, True), shares(number_of, rows * top, reach, slope, False)
    places = jnp.arange(number_of)

    def named(lengths, rotation):
        used = int((lengths > 0).sum())
        fixed = max(1, used // 4)
        moved = fixed + (places - fixed + rotation * (used - fixed)) % max(1, number_of - fixed)
        return jnp.zeros((number_of,), jnp.int32).at[sequence[jnp.where(places < fixed, places, moved)]].set(jnp.asarray(lengths, jnp.int32))

    lengths = jnp.where(number % 4 == 0, named(crowded, number // 4), named(common, number - number // 4 - 1))
    mixed = jax.random.permutation(jax.random.fold_in(own, 3), number_of)
    donor, taker = mixed[0:number_of // 2 * 2:2], mixed[1:number_of // 2 * 2:2]
    room = jnp.minimum(lengths[donor] - 1, reach - lengths[taker]) // 2
    room = jnp.where((donor == sequence[0]) | (taker == sequence[0]) | (lengths[taker] == 0), 0, jnp.maximum(room, 0))
    moved = jax.random.randint(jax.random.fold_in(own, 4), (number_of // 2,), 0, 1 << 20) % (room + 1)
    lengths = lengths.at[donor].add(-moved).at[taker].add(moved)
    members = jnp.searchsorted(jnp.cumsum(lengths), jnp.arange(rows * top), side="right").astype(jnp.int32)
    table = members.reshape(top, rows).T
    table = table[jax.random.permutation(jax.random.fold_in(own, 1), rows)]
    rotation = jax.random.randint(jax.random.fold_in(own, 2), (rows, 1), 0, top)
    return jnp.take_along_axis(table, (jnp.arange(top)[None, :] + rotation) % top, axis=1)


def shares(amount, total, bound, lean, full):
    portions = [(1 << 20) // math.isqrt(standing ** lean) + 1 for standing in range(1, amount + 1)]
    largest = bound if full else min(bound, max(-(-total // amount), total * portions[0] // sum(portions)))
    least = 1 if total - largest >= amount - 1 else 0
    given, rest = [largest] + [least] * (amount - 1), total - largest - least * (amount - 1)
    while rest > 0:
        candidates = [i for i in range(1, amount) if given[i] < largest] or [i for i in range(1, amount) if given[i] < bound]
        pool, budget = sum([portions[i] for i in candidates]), rest
        for i in candidates:
            more = min(bound - given[i], max(1, budget * portions[i] // pool), rest)
            given[i] = given[i] + more
            rest = rest - more
    return np.array(given)


def normal_values(rng, extent, width, limit, split=(), kind=jnp.bfloat16):
    factor_of = block_scale(rng, extent, split, -0.22, 0.18) if split else 1.0
    drawn = jax.random.normal(rng, extent, jnp.float32) * width * factor_of
    return jnp.minimum(jnp.maximum(drawn, -limit), limit).astype(kind)


def setup_inputs(seed: int = 0) -> dict:
    streams_of = jax.random.split(jax.random.key(seed), 14)
    hidden = normal_values(streams_of[0], (BATCH, SEQ, D), 1.0, 6.0, ((0, 32), (1, 8)))
    queries = draw_queries(jax.random.fold_in(streams_of[13], 71), 0)
    latent = draw_latent(jax.random.fold_in(streams_of[13], 71), 0)
    group_order = jax.random.permutation(streams_of[3], 2 * N_CTX).astype(jnp.int32)
    w_uk = normal_values(streams_of[4], (KVR, HEADS * NOPE), KVR ** -0.5, 0.25)
    w_uv = normal_values(streams_of[5], (KVR, HEADS * VDIM), KVR ** -0.5, 0.25)
    w_out = normal_values(streams_of[6], (HEADS * VDIM, D), (HEADS * VDIM) ** -0.5, 0.1875)
    norm_gain = jnp.clip(1.0 + 0.1 * jax.random.normal(streams_of[7], (D,), jnp.float32), 0.5, 1.5)
    expert_ids_keys = jax.random.split(jax.random.fold_in(streams_of[8], 1), BATCH * SEQ // TOK_DEV)
    expert_ids_turns = jax.random.permutation(jax.random.fold_in(streams_of[8], 3), BATCH * SEQ // TOK_DEV)
    expert_ids = jax.vmap(lambda own, number: assign_block(jax.random.fold_in(streams_of[8], 2), own, number, TOK_DEV, EXPERTS, TOPK, CAP, 1))(expert_ids_keys, expert_ids_turns).reshape((BATCH, SEQ, TOPK))
    gate_weights = jnp.clip(0.05 + 0.45 * jax.random.uniform(streams_of[9], (BATCH, SEQ, TOPK), jnp.float32) ** block_scale(streams_of[9], (BATCH, SEQ, TOPK), ((0, 32), (1, 8)), -0.2, 0.2), 0.05, 0.5)
    w_gate = normal_values(streams_of[10], (EXPERTS, D, MOE_FF), D ** -0.5, 0.125, ((0, 32), (2, 8)))
    w_up = normal_values(streams_of[11], (EXPERTS, D, MOE_FF), D ** -0.5, 0.125, ((0, 32), (2, 8)))
    w_down = normal_values(streams_of[12], (EXPERTS, D, MOE_FF), MOE_FF ** -0.5, 0.1875, ((0, 32), (2, 8)))
    return dict(hidden=hidden, queries=queries, latent=latent, group_order=group_order, w_uk=w_uk, w_uv=w_uv, w_out=w_out, norm_gain=norm_gain, expert_ids=expert_ids, gate_weights=gate_weights, w_gate=w_gate, w_up=w_up, w_down=w_down)


EPSILON = 1e-06

def layout_positions(group_order, half_rows, seq_rows):
    row_index = jnp.arange(seq_rows, dtype=jnp.int32)
    return group_order[row_index // half_rows] * half_rows + row_index % half_rows

def block_slots(block_ids):
    flat_ids = block_ids.reshape(-1)
    onehot = (flat_ids[:, None] == jnp.arange(EXPERTS, dtype=jnp.int32)[None, :]).astype(jnp.int32)
    before = lax.optimization_barrier(jnp.sum((jnp.cumsum(onehot, axis=0) - onehot) * onehot, axis=1))
    return (flat_ids * CAP + before).astype(jnp.int32)

def attention_layer(hidden_rows, query_rows, latent_rows, positions, w_uk, w_uv, w_out, norm_gain):
    content = latent_rows[:, :KVR]
    key_rope = latent_rows[:, KVR:].astype(jnp.float32)
    key_nope = jnp.dot(content, w_uk, preferred_element_type=jnp.float32).astype(jnp.bfloat16)
    values = jnp.dot(content, w_uv, preferred_element_type=jnp.float32).astype(jnp.bfloat16)
    query_full = query_rows.astype(jnp.float32).reshape(SEQ, HEADS, NOPE + ROPE)
    scores = jnp.einsum('qhd,khd->hqk', query_full[:, :, :NOPE], key_nope.astype(jnp.float32).reshape(SEQ, HEADS, NOPE))
    scores = scores + jnp.einsum('qhr,kr->hqk', query_full[:, :, NOPE:], key_rope)
    scores = scores * (NOPE + ROPE) ** (-0.5)
    visible = positions[None, :] <= positions[:, None]
    scores = jnp.where(visible[None], scores, -jnp.inf)
    peak = lax.optimization_barrier(jnp.max(scores, axis=2, keepdims=True))
    expo = jnp.exp(scores - peak)
    totals = lax.optimization_barrier(jnp.sum(expo, axis=2))
    rounded = lax.optimization_barrier(expo.astype(jnp.bfloat16)).astype(jnp.float32)
    heads_out = jnp.einsum('hqk,khv->qhv', rounded, values.astype(jnp.float32).reshape(SEQ, HEADS, VDIM))
    heads_out = heads_out / jnp.transpose(totals)[:, :, None]
    attended = heads_out.astype(jnp.bfloat16).reshape(SEQ, HEADS * VDIM)
    residual = (hidden_rows.astype(jnp.float32) + jnp.dot(attended, w_out, preferred_element_type=jnp.float32)).astype(jnp.bfloat16)
    stream = lax.optimization_barrier(residual).astype(jnp.float32)
    factor = lax.rsqrt(lax.optimization_barrier(jnp.mean(stream * stream, axis=1, keepdims=True)) + EPSILON)
    normed = (stream * factor * norm_gain.astype(jnp.float32)).astype(jnp.bfloat16)
    return (residual, normed)

def reference(hidden, queries, latent, group_order, w_uk, w_uv, w_out, norm_gain, expert_ids, gate_weights, w_gate, w_up, w_down):
    positions = layout_positions(group_order, HALF, SEQ)

    def per_sequence(items):
        hidden_rows, query_rows, latent_rows = items
        return attention_layer(hidden_rows, query_rows, latent_rows, positions, w_uk, w_uv, w_out, norm_gain)
    residual, normed = lax.map(per_sequence, (hidden, queries, latent))
    blocks = BATCH * N_CTX
    total_rows = blocks * TOK_DEV
    normed_flat = jnp.concatenate([normed.reshape(total_rows, D), jnp.zeros((1, D), normed.dtype)], axis=0)
    id_blocks = expert_ids.reshape(blocks, TOK_DEV, TOPK)
    gate_blocks = gate_weights.reshape(blocks, TOK_DEV * TOPK)
    slots = jax.vmap(block_slots)(id_blocks)

    def invert_block(slot_index, gates, block):
        token_index = block * TOK_DEV + jnp.arange(TOK_DEV * TOPK, dtype=jnp.int32) // TOPK
        owners = jnp.full((EXPERTS * CAP,), total_rows, jnp.int32).at[slot_index].set(token_index.astype(jnp.int32))
        weights = jnp.zeros((EXPERTS * CAP,), gates.dtype).at[slot_index].set(gates)
        return (owners, weights)
    owners, slot_gates = jax.vmap(invert_block)(slots, gate_blocks, jnp.arange(blocks, dtype=jnp.int32))
    owners = owners.reshape(blocks, EXPERTS, CAP)
    slot_gates = slot_gates.reshape(blocks, EXPERTS, CAP)

    def run_expert(accum, expert):
        token_rows = lax.dynamic_index_in_dim(owners, expert, axis=1, keepdims=False).reshape(-1)
        gates = lax.dynamic_index_in_dim(slot_gates, expert, axis=1, keepdims=False).reshape(-1)
        rows = normed_flat[token_rows]
        gate_part = jnp.dot(rows, w_gate[expert], preferred_element_type=jnp.float32)
        up_part = jnp.dot(rows, w_up[expert], preferred_element_type=jnp.float32)
        inner = (jax.nn.silu(gate_part) * up_part).astype(jnp.bfloat16)
        output = jnp.dot(inner, jnp.transpose(w_down[expert]), preferred_element_type=jnp.float32).astype(jnp.bfloat16)
        accum = accum.at[token_rows].add(gates[:, None] * output.astype(jnp.float32))
        return (accum, None)
    start = jnp.zeros((total_rows + 1, D), jnp.float32)
    accum, unused = lax.scan(run_expert, start, jnp.arange(EXPERTS, dtype=jnp.int32))
    mixed = residual.reshape(total_rows, D).astype(jnp.float32) + accum[:total_rows]
    return mixed.astype(jnp.bfloat16).reshape(BATCH, SEQ, D)
```

```python
import jax
import jax.numpy as jnp
from jax import lax
from jax.experimental import pallas as pl
from jax.experimental.pallas import tpu as pltpu
from jax.sharding import PartitionSpec as P

D = 2048
HEADS = 8
NOPE = 128
ROPE = 64
VDIM = 128
KVR = 512
EXPERTS = 64
TOPK = 6
CAP = 13
EPSILON = 1e-06

CHUNKS = 4
WIDTH = D // CHUNKS
LOCAL = 2
GROUP = LOCAL * CHUNKS
BLOCK = CAP * GROUP
PACK = 16
FF_BLOCK = 512
MIB = 1 << 20


def whole_vmem():
    return pl.BlockSpec(memory_space=pltpu.VMEM)


def gather_directly(shard, axis):
    length = lax.axis_size(axis)
    return lax.all_to_all(
        jnp.broadcast_to(shard[None], (length, *shard.shape)), axis, 0, 0, tiled=True
    ).reshape(length * shard.shape[0], *shard.shape[1:])


def routing(ids, gates):
    rows = ids.shape[0]
    chosen = ids[:, :, None] == jnp.arange(EXPERTS, dtype=jnp.int32)[None, None, :]
    named = jnp.any(chosen, axis=1)
    gate_of = jnp.sum(jnp.where(chosen, gates[:, :, None], 0.0), axis=1)
    order = jnp.arange(rows, dtype=jnp.int32)
    earlier = (order[None, :] < order[:, None]).astype(jnp.bfloat16)
    before = jnp.dot(earlier, named.astype(jnp.bfloat16), preferred_element_type=jnp.float32)
    rank_of = jnp.where(named, before, -1.0).astype(jnp.bfloat16)
    return rank_of, gate_of


def selectors(ids, gates, peers):
    rank_of, gate_of = routing(ids, gates)
    total = peers * BLOCK
    row = jnp.arange(total, dtype=jnp.int32)
    expert = (row // BLOCK) * LOCAL + (row // CHUNKS) % LOCAL
    rank = ((row % BLOCK) // GROUP).astype(jnp.float32)
    onehot = (expert[:, None] == jnp.arange(EXPERTS, dtype=jnp.int32)[None, :]).astype(jnp.bfloat16)
    at_rows = lax.dot_general(
        onehot, rank_of, (((1,), (1,)), ((), ())), preferred_element_type=jnp.float32
    )
    send = (at_rows == rank[:, None]).astype(jnp.bfloat16)
    at_cols = lax.dot_general(
        rank_of, onehot, (((1,), (1,)), ((), ())), preferred_element_type=jnp.float32
    )
    gate_cols = lax.dot_general(
        gate_of.astype(jnp.bfloat16),
        onehot,
        (((1,), (1,)), ((), ())),
        preferred_element_type=jnp.float32,
    )
    combine = jnp.where(at_cols == rank[None, :], gate_cols, 0.0).astype(jnp.bfloat16)
    return send, combine


def send_kernel(select_ref, rows_ref, out_ref):
    select = select_ref[...]
    which = lax.broadcasted_iota(jnp.int32, select.shape, 0) % CHUNKS
    parts = [jnp.where(which == j, select, jnp.zeros_like(select)) for j in range(CHUNKS)]
    left = jnp.concatenate(parts, axis=1)
    right = jnp.concatenate(
        [rows_ref[:, j * WIDTH : (j + 1) * WIDTH] for j in range(CHUNKS)], axis=0
    )
    out_ref[...] = jnp.dot(left, right, preferred_element_type=jnp.float32).astype(jnp.bfloat16)


def send_rows(select, rows):
    total, tokens = select.shape
    step = total // 8
    return pl.pallas_call(
        send_kernel,
        out_shape=jax.ShapeDtypeStruct((total, WIDTH), jnp.bfloat16),
        grid=(8,),
        in_specs=[
            pl.BlockSpec((step, tokens), lambda i: (i, 0)),
            pl.BlockSpec((tokens, D), lambda i: (0, 0)),
        ],
        out_specs=pl.BlockSpec((step, WIDTH), lambda i: (i, 0)),
        compiler_params=pltpu.CompilerParams(vmem_limit_bytes=24 * MIB),
        name="send_rows",
    )(select, rows)


def pack_matrix(transposed):
    side = PACK * GROUP
    a = lax.broadcasted_iota(jnp.int32, (side, side), 1 if transposed else 0)
    b = lax.broadcasted_iota(jnp.int32, (side, side), 0 if transposed else 1)
    return (b == (a % PACK) * GROUP + a // PACK).astype(jnp.float32).astype(jnp.bfloat16)


def expert_kernel(recv_ref, gate_ref, up_ref, down_ref, out_ref, x_ref, acc_ref, y_ref):
    expert, part = pl.program_id(0), pl.program_id(1)
    parts = pl.num_programs(1)
    side = PACK * GROUP
    blocks = recv_ref.shape[0] // side

    @pl.when((expert == 0) & (part == 0))
    def _():
        unpack = pack_matrix(False)
        for b in range(blocks):
            got = jnp.dot(
                unpack,
                recv_ref[b * side : (b + 1) * side, :],
                preferred_element_type=jnp.float32,
            ).astype(jnp.bfloat16)
            for k in range(LOCAL):
                for j in range(CHUNKS):
                    at = (k * CHUNKS + j) * PACK
                    x_ref[k, b * PACK : (b + 1) * PACK, j * WIDTH : (j + 1) * WIDTH] = got[
                        at : at + PACK, :
                    ]

    x = x_ref[expert]
    gate = jnp.dot(x, gate_ref[0], preferred_element_type=jnp.float32)
    up = jnp.dot(x, up_ref[0], preferred_element_type=jnp.float32)
    inner = (gate / (1.0 + jnp.exp(-gate)) * up).astype(jnp.bfloat16)
    out = lax.dot_general(
        inner, down_ref[0], (((1,), (1,)), ((), ())), preferred_element_type=jnp.float32
    )

    @pl.when(part == 0)
    def _():
        acc_ref[...] = out

    @pl.when((part > 0) & (part < parts - 1))
    def _():
        acc_ref[...] += out

    @pl.when(part == parts - 1)
    def _():
        y_ref[expert] = (acc_ref[...] + out).astype(jnp.bfloat16)

    @pl.when((expert == LOCAL - 1) & (part == parts - 1))
    def _():
        pack = pack_matrix(True)
        for b in range(blocks):
            pieces = [
                y_ref[k, b * PACK : (b + 1) * PACK, j * WIDTH : (j + 1) * WIDTH]
                for k in range(LOCAL)
                for j in range(CHUNKS)
            ]
            out_ref[b * side : (b + 1) * side, :] = jnp.dot(
                pack, jnp.concatenate(pieces, axis=0), preferred_element_type=jnp.float32
            ).astype(jnp.bfloat16)


def run_experts(received, weights):
    total = received.shape[0]
    items = total // GROUP
    hidden_units = weights.shape[2]
    return pl.pallas_call(
        expert_kernel,
        out_shape=jax.ShapeDtypeStruct(received.shape, jnp.bfloat16),
        grid=(LOCAL, hidden_units // FF_BLOCK),
        in_specs=[
            pl.BlockSpec((total, WIDTH), lambda k, f: (0, 0), pipeline_mode=pl.Buffered(1)),
            pl.BlockSpec((1, D, FF_BLOCK), lambda k, f: (k, 0, f)),
            pl.BlockSpec((1, D, FF_BLOCK), lambda k, f: (LOCAL + k, 0, f)),
            pl.BlockSpec((1, D, FF_BLOCK), lambda k, f: (2 * LOCAL + k, 0, f)),
        ],
        out_specs=pl.BlockSpec((total, WIDTH), lambda k, f: (0, 0), pipeline_mode=pl.Buffered(1)),
        scratch_shapes=[
            pltpu.VMEM((LOCAL, items, D), jnp.bfloat16),
            pltpu.VMEM((items, D), jnp.float32),
            pltpu.VMEM((LOCAL, items, D), jnp.bfloat16),
        ],
        compiler_params=pltpu.CompilerParams(vmem_limit_bytes=52 * MIB),
        name="run_experts",
    )(received, weights, weights, weights)


def combine_kernel(combine_ref, rows_ref, residual_ref, out_ref):
    combine = combine_ref[...]
    which = lax.broadcasted_iota(jnp.int32, combine.shape, 1) % CHUNKS
    left = jnp.concatenate(
        [jnp.where(which == j, combine, jnp.zeros_like(combine)) for j in range(CHUNKS)], axis=0
    )
    got = jnp.dot(left, rows_ref[...], preferred_element_type=jnp.float32)
    tokens = combine.shape[0]
    for j in range(CHUNKS):
        cols = slice(j * WIDTH, (j + 1) * WIDTH)
        out_ref[:, cols] = (
            residual_ref[:, cols].astype(jnp.float32) + got[j * tokens : (j + 1) * tokens, :]
        ).astype(jnp.bfloat16)


def combine_rows(combine, rows, residual):
    return pl.pallas_call(
        combine_kernel,
        out_shape=jax.ShapeDtypeStruct(residual.shape, jnp.bfloat16),
        in_specs=[whole_vmem(), whole_vmem(), whole_vmem()],
        out_specs=whole_vmem(),
        compiler_params=pltpu.CompilerParams(vmem_limit_bytes=32 * MIB),
        name="combine_rows",
    )(combine, rows, residual)


def body(
    hidden,
    queries,
    latent,
    group_order,
    w_uk,
    w_uv,
    w_out,
    norm_gain,
    expert_ids,
    gate_weights,
    w_gate,
    w_up,
    w_down,
):
    peers = lax.axis_size("exp")
    block_rows = hidden.shape[1]
    half_rows = block_rows // 2
    seq_rows = block_rows * lax.axis_size("ctx")
    whole = gather_directly(latent[0], "ctx")
    weights = lax.all_gather(
        jnp.concatenate([w_gate, w_up, w_down], axis=0), "ctx", axis=2, tiled=True
    )
    row_index = jnp.arange(seq_rows, dtype=jnp.int32)
    positions = group_order[row_index // half_rows] * half_rows + row_index % half_rows
    own_positions = lax.dynamic_slice_in_dim(
        positions, lax.axis_index("ctx") * block_rows, block_rows
    )
    send, combine = selectors(expert_ids[0], gate_weights[0], peers)

    content = whole[:, :KVR]
    key_rope = whole[:, KVR:]
    key_nope = jnp.dot(content, w_uk, preferred_element_type=jnp.float32).astype(jnp.bfloat16)
    values = jnp.dot(content, w_uv, preferred_element_type=jnp.float32).astype(jnp.bfloat16)
    query_full = queries[0].reshape(block_rows, HEADS, NOPE + ROPE)
    scores = jnp.einsum(
        "qhd,khd->hqk",
        query_full[:, :, :NOPE],
        key_nope.reshape(seq_rows, HEADS, NOPE),
        preferred_element_type=jnp.float32,
    )
    scores = scores + jnp.einsum(
        "qhr,kr->hqk", query_full[:, :, NOPE:], key_rope, preferred_element_type=jnp.float32
    )
    scores = scores * (NOPE + ROPE) ** (-0.5)
    visible = positions[None, :] <= own_positions[:, None]
    scores = jnp.where(visible[None], scores, -jnp.inf)
    peak = jnp.max(scores, axis=2, keepdims=True)
    expo = jnp.exp(scores - peak)
    totals = jnp.sum(expo, axis=2)
    heads_out = jnp.einsum(
        "hqk,khv->qhv",
        expo.astype(jnp.bfloat16),
        values.reshape(seq_rows, HEADS, VDIM),
        preferred_element_type=jnp.float32,
    )
    heads_out = heads_out / jnp.transpose(totals)[:, :, None]
    attended = heads_out.astype(jnp.bfloat16).reshape(block_rows, HEADS * VDIM)
    residual = (
        hidden[0].astype(jnp.float32) + jnp.dot(attended, w_out, preferred_element_type=jnp.float32)
    ).astype(jnp.bfloat16)
    stream = residual.astype(jnp.float32)
    factor = lax.rsqrt(jnp.mean(stream * stream, axis=1, keepdims=True) + EPSILON)
    normed = (stream * factor * norm_gain).astype(jnp.bfloat16)

    outgoing = send_rows(send, normed).reshape(peers, BLOCK, WIDTH)
    received = lax.all_to_all(outgoing, "exp", split_axis=0, concat_axis=0, tiled=True)
    done = run_experts(received.reshape(peers * BLOCK, WIDTH), weights)
    returned = lax.all_to_all(
        done.reshape(peers, BLOCK, WIDTH), "exp", split_axis=0, concat_axis=0, tiled=True
    )
    return combine_rows(combine, returned.reshape(peers * BLOCK, WIDTH), residual)[None]


def solution(mesh):
    return jax.shard_map(
        body,
        mesh=mesh,
        in_specs=(
            P("exp", "ctx", None),
            P("exp", "ctx", None),
            P("exp", "ctx", None),
            P(),
            P(),
            P(),
            P(),
            P(),
            P("exp", "ctx", None),
            P("exp", "ctx", None),
            P("exp", None, "ctx"),
            P("exp", None, "ctx"),
            P("exp", None, "ctx"),
        ),
        out_specs=P("exp", "ctx", None),
        check_vma=False,
    )
```

```python
import jax
import jax.numpy as jnp
from jax import lax
from jax.experimental import pallas as pl
from jax.experimental.pallas import tpu as pltpu
from jax.sharding import PartitionSpec as P

D = 2048
HEADS = 8
NOPE = 128
ROPE = 64
VDIM = 128
KVR = 512
EXPERTS = 64
TOPK = 6
CAP = 13
EPSILON = 1e-06

CHUNKS = 8
WIDTH = D // CHUNKS
LOCAL = 2
BLOCK = CAP * CHUNKS
PACK = 16
FF_BLOCK = 256
MIB = 1 << 20


def whole_vmem():
    return pl.BlockSpec(memory_space=pltpu.VMEM)


def gather_directly(shard, axis):
    length = lax.axis_size(axis)
    return lax.all_to_all(
        jnp.broadcast_to(shard[None], (length, *shard.shape)), axis, 0, 0, tiled=True
    ).reshape(length * shard.shape[0], *shard.shape[1:])


def exchanged(rows, peers):
    return lax.all_to_all(
        rows.reshape(peers, BLOCK, WIDTH), "exp", split_axis=0, concat_axis=0, tiled=True
    ).reshape(peers * BLOCK, WIDTH)


def routing(ids, gates):
    rows = ids.shape[0]
    chosen = ids[:, :, None] == jnp.arange(EXPERTS, dtype=jnp.int32)[None, None, :]
    named = jnp.any(chosen, axis=1)
    gate_of = jnp.sum(jnp.where(chosen, gates[:, :, None], 0.0), axis=1)
    order = jnp.arange(rows, dtype=jnp.int32)
    earlier = (order[None, :] < order[:, None]).astype(jnp.bfloat16)
    before = jnp.dot(earlier, named.astype(jnp.bfloat16), preferred_element_type=jnp.float32)
    rank_of = jnp.where(named, before, -1.0).astype(jnp.bfloat16)
    return rank_of, gate_of


def selectors(rank_of, gate_of, local, peers):
    total = peers * BLOCK
    row = jnp.arange(total, dtype=jnp.int32)
    expert = (row // BLOCK) * LOCAL + local
    rank = ((row % BLOCK) // CHUNKS).astype(jnp.float32)
    onehot = (expert[:, None] == jnp.arange(EXPERTS, dtype=jnp.int32)[None, :]).astype(jnp.bfloat16)
    at_rows = lax.dot_general(
        onehot, rank_of, (((1,), (1,)), ((), ())), preferred_element_type=jnp.float32
    )
    send = (at_rows == rank[:, None]).astype(jnp.bfloat16)
    at_cols = lax.dot_general(
        rank_of, onehot, (((1,), (1,)), ((), ())), preferred_element_type=jnp.float32
    )
    gate_cols = lax.dot_general(
        gate_of.astype(jnp.bfloat16),
        onehot,
        (((1,), (1,)), ((), ())),
        preferred_element_type=jnp.float32,
    )
    combine = jnp.where(at_cols == rank[None, :], gate_cols, 0.0).astype(jnp.bfloat16)
    return send, combine


def send_kernel(select_ref, rows_ref, out_ref):
    select = select_ref[...]
    which = lax.broadcasted_iota(jnp.int32, select.shape, 0) % CHUNKS
    parts = [jnp.where(which == j, select, jnp.zeros_like(select)) for j in range(CHUNKS)]
    left = jnp.concatenate(parts, axis=1)
    right = jnp.concatenate(
        [rows_ref[:, j * WIDTH : (j + 1) * WIDTH] for j in range(CHUNKS)], axis=0
    )
    out_ref[...] = jnp.dot(left, right, preferred_element_type=jnp.float32).astype(jnp.bfloat16)


def send_rows(select, rows):
    total, tokens = select.shape
    step = total // 8
    return pl.pallas_call(
        send_kernel,
        out_shape=jax.ShapeDtypeStruct((total, WIDTH), jnp.bfloat16),
        grid=(8,),
        in_specs=[
            pl.BlockSpec((step, tokens), lambda i: (i, 0)),
            pl.BlockSpec((tokens, D), lambda i: (0, 0)),
        ],
        out_specs=pl.BlockSpec((step, WIDTH), lambda i: (i, 0)),
        compiler_params=pltpu.CompilerParams(vmem_limit_bytes=24 * MIB),
        name="send_rows",
    )(select, rows)


def pack_matrix(transposed):
    side = PACK * CHUNKS
    a = lax.broadcasted_iota(jnp.int32, (side, side), 1 if transposed else 0)
    b = lax.broadcasted_iota(jnp.int32, (side, side), 0 if transposed else 1)
    return (b == (a % PACK) * CHUNKS + a // PACK).astype(jnp.float32).astype(jnp.bfloat16)


def expert_kernel(recv_ref, gate_ref, up_ref, down_ref, out_ref, x_ref, acc_ref):
    part = pl.program_id(0)
    parts = pl.num_programs(0)
    side = PACK * CHUNKS
    blocks = recv_ref.shape[0] // side

    @pl.when(part == 0)
    def _():
        unpack = pack_matrix(False)
        for b in range(blocks):
            got = jnp.dot(
                unpack,
                recv_ref[b * side : (b + 1) * side, :],
                preferred_element_type=jnp.float32,
            ).astype(jnp.bfloat16)
            for j in range(CHUNKS):
                x_ref[b * PACK : (b + 1) * PACK, j * WIDTH : (j + 1) * WIDTH] = got[
                    j * PACK : (j + 1) * PACK, :
                ]

    x = x_ref[...]
    gate = jnp.dot(x, gate_ref[0], preferred_element_type=jnp.float32)
    up = jnp.dot(x, up_ref[0], preferred_element_type=jnp.float32)
    inner = (gate / (1.0 + jnp.exp(-gate)) * up).astype(jnp.bfloat16)
    out = lax.dot_general(
        inner, down_ref[0], (((1,), (1,)), ((), ())), preferred_element_type=jnp.float32
    )

    @pl.when(part == 0)
    def _():
        acc_ref[...] = out

    @pl.when((part > 0) & (part < parts - 1))
    def _():
        acc_ref[...] += out

    @pl.when(part == parts - 1)
    def _():
        x_ref[...] = (acc_ref[...] + out).astype(jnp.bfloat16)
        pack = pack_matrix(True)
        for b in range(blocks):
            pieces = [
                x_ref[b * PACK : (b + 1) * PACK, j * WIDTH : (j + 1) * WIDTH]
                for j in range(CHUNKS)
            ]
            out_ref[b * side : (b + 1) * side, :] = jnp.dot(
                pack, jnp.concatenate(pieces, axis=0), preferred_element_type=jnp.float32
            ).astype(jnp.bfloat16)


def run_expert(received, weights):
    total = received.shape[0]
    items = total // CHUNKS
    hidden_units = weights.shape[2]
    return pl.pallas_call(
        expert_kernel,
        out_shape=jax.ShapeDtypeStruct(received.shape, jnp.bfloat16),
        grid=(hidden_units // FF_BLOCK,),
        in_specs=[
            pl.BlockSpec((total, WIDTH), lambda f: (0, 0), pipeline_mode=pl.Buffered(1)),
            pl.BlockSpec((1, D, FF_BLOCK), lambda f: (0, 0, f)),
            pl.BlockSpec((1, D, FF_BLOCK), lambda f: (1, 0, f)),
            pl.BlockSpec((1, D, FF_BLOCK), lambda f: (2, 0, f)),
        ],
        out_specs=pl.BlockSpec((total, WIDTH), lambda f: (0, 0), pipeline_mode=pl.Buffered(1)),
        scratch_shapes=[
            pltpu.VMEM((items, D), jnp.bfloat16),
            pltpu.VMEM((items, D), jnp.float32),
        ],
        compiler_params=pltpu.CompilerParams(vmem_limit_bytes=36 * MIB),
        name="run_expert",
    )(received, weights, weights, weights)


def combine_kernel(combine_ref, rows_ref, residual_ref, out_ref):
    combine = combine_ref[...]
    which = lax.broadcasted_iota(jnp.int32, combine.shape, 1) % CHUNKS
    left = jnp.concatenate(
        [jnp.where(which == j, combine, jnp.zeros_like(combine)) for j in range(CHUNKS)], axis=0
    )
    got = jnp.dot(left, rows_ref[...], preferred_element_type=jnp.float32)
    tokens = combine.shape[0]
    for j in range(CHUNKS):
        cols = slice(j * WIDTH, (j + 1) * WIDTH)
        out_ref[:, cols] = (
            residual_ref[:, cols].astype(jnp.float32) + got[j * tokens : (j + 1) * tokens, :]
        ).astype(out_ref.dtype)


def combine_rows(combine, rows, residual, dtype):
    return pl.pallas_call(
        combine_kernel,
        out_shape=jax.ShapeDtypeStruct(residual.shape, dtype),
        in_specs=[whole_vmem(), whole_vmem(), whole_vmem()],
        out_specs=whole_vmem(),
        compiler_params=pltpu.CompilerParams(vmem_limit_bytes=32 * MIB),
        name="combine_rows",
    )(combine, rows, residual)


def body(
    hidden,
    queries,
    latent,
    group_order,
    w_uk,
    w_uv,
    w_out,
    norm_gain,
    expert_ids,
    gate_weights,
    w_gate,
    w_up,
    w_down,
):
    peers = lax.axis_size("exp")
    block_rows = hidden.shape[1]
    half_rows = block_rows // 2
    seq_rows = block_rows * lax.axis_size("ctx")
    whole = gather_directly(latent[0], "ctx")
    weights = [
        lax.all_gather(
            jnp.stack([w_gate[k], w_up[k], w_down[k]]), "ctx", axis=2, tiled=True
        )
        for k in range(LOCAL)
    ]
    row_index = jnp.arange(seq_rows, dtype=jnp.int32)
    positions = group_order[row_index // half_rows] * half_rows + row_index % half_rows
    own_positions = lax.dynamic_slice_in_dim(
        positions, lax.axis_index("ctx") * block_rows, block_rows
    )
    rank_of, gate_of = routing(expert_ids[0], gate_weights[0])
    plans = [selectors(rank_of, gate_of, k, peers) for k in range(LOCAL)]

    content = whole[:, :KVR]
    key_rope = whole[:, KVR:]
    key_nope = jnp.dot(content, w_uk, preferred_element_type=jnp.float32).astype(jnp.bfloat16)
    values = jnp.dot(content, w_uv, preferred_element_type=jnp.float32).astype(jnp.bfloat16)
    query_full = queries[0].reshape(block_rows, HEADS, NOPE + ROPE)
    scores = jnp.einsum(
        "qhd,khd->hqk",
        query_full[:, :, :NOPE],
        key_nope.reshape(seq_rows, HEADS, NOPE),
        preferred_element_type=jnp.float32,
    )
    scores = scores + jnp.einsum(
        "qhr,kr->hqk", query_full[:, :, NOPE:], key_rope, preferred_element_type=jnp.float32
    )
    scores = scores * (NOPE + ROPE) ** (-0.5)
    visible = positions[None, :] <= own_positions[:, None]
    scores = jnp.where(visible[None], scores, -jnp.inf)
    peak = jnp.max(scores, axis=2, keepdims=True)
    expo = jnp.exp(scores - peak)
    totals = jnp.sum(expo, axis=2)
    heads_out = jnp.einsum(
        "hqk,khv->qhv",
        expo.astype(jnp.bfloat16),
        values.reshape(seq_rows, HEADS, VDIM),
        preferred_element_type=jnp.float32,
    )
    heads_out = heads_out / jnp.transpose(totals)[:, :, None]
    attended = heads_out.astype(jnp.bfloat16).reshape(block_rows, HEADS * VDIM)
    residual = (
        hidden[0].astype(jnp.float32) + jnp.dot(attended, w_out, preferred_element_type=jnp.float32)
    ).astype(jnp.bfloat16)
    stream = residual.astype(jnp.float32)
    factor = lax.rsqrt(jnp.mean(stream * stream, axis=1, keepdims=True) + EPSILON)
    normed = (stream * factor * norm_gain).astype(jnp.bfloat16)

    received = []
    for k in range(LOCAL):
        outgoing = send_rows(plans[k][0], normed)
        if received:
            outgoing, _ = lax.optimization_barrier((outgoing, received[-1]))
        received.append(exchanged(outgoing, peers))
    mixed = residual
    returned = [exchanged(run_expert(received[k], weights[k]), peers) for k in range(LOCAL)]
    for k in range(LOCAL):
        last = k == LOCAL - 1
        mixed = combine_rows(plans[k][1], returned[k], mixed, jnp.bfloat16 if last else jnp.float32)
    return mixed[None]


def solution(mesh):
    return jax.shard_map(
        body,
        mesh=mesh,
        in_specs=(
            P("exp", "ctx", None),
            P("exp", "ctx", None),
            P("exp", "ctx", None),
            P(),
            P(),
            P(),
            P(),
            P(),
            P("exp", "ctx", None),
            P("exp", "ctx", None),
            P("exp", None, "ctx"),
            P("exp", None, "ctx"),
            P("exp", None, "ctx"),
        ),
        out_specs=P("exp", "ctx", None),
        check_vma=False,
    )
```

```python
import jax
import jax.numpy as jnp
from jax import lax
from jax.experimental import pallas as pl
from jax.experimental.pallas import tpu as pltpu
from jax.sharding import Mesh
from jax.sharding import PartitionSpec as P

D = 2048
HEADS = 8
NOPE = 128
ROPE = 64
VDIM = 128
KVR = 512
EXPERTS = 64
TOPK = 6
CAP = 13
EPSILON = 1e-06

CHUNKS = 8
WIDTH = D // CHUNKS
LOCAL = 2
BLOCK = CAP * CHUNKS
PACK = 16
FF_BLOCK = 256
MIB = 1 << 20

EXTRA = 128
NEAR = 2
PAIR = LOCAL * CAP


def whole_vmem():
    return pl.BlockSpec(memory_space=pltpu.VMEM)


def gather_directly(shard, axis):
    length = lax.axis_size(axis)
    return lax.all_to_all(
        jnp.broadcast_to(shard[None], (length, *shard.shape)), axis, 0, 0, tiled=True
    ).reshape(length * shard.shape[0], *shard.shape[1:])


def exchanged(rows, peers):
    return lax.all_to_all(
        rows.reshape(peers, BLOCK, WIDTH), ("x", "z"), split_axis=0, concat_axis=0, tiled=True
    ).reshape(peers * BLOCK, WIDTH)


def routing(ids, gates):
    rows = ids.shape[0]
    chosen = ids[:, :, None] == jnp.arange(EXPERTS, dtype=jnp.int32)[None, None, :]
    named = jnp.any(chosen, axis=1)
    gate_of = jnp.sum(jnp.where(chosen, gates[:, :, None], 0.0), axis=1)
    order = jnp.arange(rows, dtype=jnp.int32)
    earlier = (order[None, :] < order[:, None]).astype(jnp.bfloat16)
    before = jnp.dot(earlier, named.astype(jnp.bfloat16), preferred_element_type=jnp.float32)
    rank_of = jnp.where(named, before, -1.0).astype(jnp.bfloat16)
    return rank_of, gate_of


def combine_weights(rank_of, gate_of, local, peers):
    total = peers * BLOCK
    row = jnp.arange(total, dtype=jnp.int32)
    expert = (row // BLOCK) * LOCAL + local
    rank = ((row % BLOCK) // CHUNKS).astype(jnp.float32)
    onehot = (expert[:, None] == jnp.arange(EXPERTS, dtype=jnp.int32)[None, :]).astype(jnp.bfloat16)
    at_cols = lax.dot_general(
        rank_of, onehot, (((1,), (1,)), ((), ())), preferred_element_type=jnp.float32
    )
    gate_cols = lax.dot_general(
        gate_of.astype(jnp.bfloat16),
        onehot,
        (((1,), (1,)), ((), ())),
        preferred_element_type=jnp.float32,
    )
    return jnp.where(at_cols == rank[None, :], gate_cols, 0.0).astype(jnp.bfloat16)


def shifted(rows, axis, by):
    length = lax.axis_size(axis)
    return lax.ppermute(rows, axis, [(i, (i + by) % length) for i in range(length)])


def group_rows(count):
    return -(-count * PAIR // 8) * 8


def pick_plan(count, ring, columns):
    rows = group_rows(count)
    row = jnp.arange(rows, dtype=jnp.int32)
    block = row // PAIR
    rank = row % CAP
    local = (row % PAIR) // CAP
    target = jnp.arange(columns, dtype=jnp.int32)
    expert = (target[:, None] * ring + lax.axis_index("z")) * LOCAL + local[None, :]
    onehot = expert[:, :, None] == jnp.arange(EXTRA, dtype=jnp.int32)[None, None, :]
    onehot = onehot.astype(jnp.bfloat16).reshape(columns * rows, EXTRA)
    wide = lambda v: jnp.broadcast_to(jnp.tile(v, columns)[:, None], (columns * rows, EXTRA))
    return onehot, wide(rank.astype(jnp.float32)), wide(block)


def pick_kernel(onehot_ref, rank_ref, block_ref, *refs):
    blocks, out_ref = refs[:-1], refs[-1]
    onehot, rank, block = onehot_ref[...], rank_ref[...], block_ref[...]
    left = []
    for p, ref in enumerate(blocks):
        at = lax.dot_general(
            onehot, ref[:, D:], (((1,), (1,)), ((), ())), preferred_element_type=jnp.float32
        )
        left.append(((at == rank) & (block == p)).astype(jnp.float32).astype(jnp.bfloat16))
    left = jnp.concatenate(left, axis=1)
    width = 512
    for c in range(0, D, width):
        right = jnp.concatenate([ref[:, c : c + width] for ref in blocks], axis=0)
        out_ref[:, c : c + width] = jnp.dot(
            left, right, preferred_element_type=jnp.float32
        ).astype(jnp.bfloat16)


def pick_rows(plan, blocks):
    return pl.pallas_call(
        pick_kernel,
        out_shape=jax.ShapeDtypeStruct((plan[0].shape[0], D), jnp.bfloat16),
        in_specs=[whole_vmem()] * (3 + len(blocks)),
        out_specs=whole_vmem(),
        compiler_params=pltpu.CompilerParams(vmem_limit_bytes=32 * MIB),
        name="pick_rows",
    )(*plan, *blocks)


def unpick_matrix(first, count, local, ring):
    rows = group_rows(count)
    out = jnp.arange(2 * ring * CAP, dtype=jnp.int32)
    source = (out // CAP) % ring
    listed = (source - lax.axis_index("z") + NEAR) % ring - first
    inside = (listed >= 0) & (listed < count)
    at = (out // (ring * CAP)) * rows + listed * PAIR + local * CAP + out % CAP
    col = jnp.arange(2 * rows, dtype=jnp.int32)
    return (inside[:, None] & (at[:, None] == col[None, :])).astype(jnp.bfloat16)


def pack_matrix():
    side = PACK * CHUNKS
    a = lax.broadcasted_iota(jnp.int32, (side, side), 1)
    b = lax.broadcasted_iota(jnp.int32, (side, side), 0)
    return (b == (a % PACK) * CHUNKS + a // PACK).astype(jnp.float32).astype(jnp.bfloat16)


def expert_kernel(
    near_ref, far_ref, near_order_ref, far_order_ref, gate_ref, up_ref, down_ref, out_ref, x_ref, acc_ref
):
    part = pl.program_id(0)
    parts = pl.num_programs(0)
    side = PACK * CHUNKS
    blocks = out_ref.shape[0] // side

    @pl.when(part == 0)
    def _():
        rows, near = near_order_ref.shape
        far = far_order_ref.shape[1]
        for i in range(x_ref.shape[0] // rows):
            got = jnp.dot(
                near_order_ref[...],
                near_ref[i * near : (i + 1) * near, :],
                preferred_element_type=jnp.float32,
            ) + jnp.dot(
                far_order_ref[...],
                far_ref[i * far : (i + 1) * far, :],
                preferred_element_type=jnp.float32,
            )
            x_ref[i * rows : (i + 1) * rows, :] = got.astype(jnp.bfloat16)

    x = x_ref[...]
    gate = jnp.dot(x, gate_ref[0], preferred_element_type=jnp.float32)
    up = jnp.dot(x, up_ref[0], preferred_element_type=jnp.float32)
    inner = (gate / (1.0 + jnp.exp(-gate)) * up).astype(jnp.bfloat16)
    out = lax.dot_general(
        inner, down_ref[0], (((1,), (1,)), ((), ())), preferred_element_type=jnp.float32
    )

    @pl.when(part == 0)
    def _():
        acc_ref[...] = out

    @pl.when((part > 0) & (part < parts - 1))
    def _():
        acc_ref[...] += out

    @pl.when(part == parts - 1)
    def _():
        x_ref[...] = (acc_ref[...] + out).astype(jnp.bfloat16)
        pack = pack_matrix()
        for b in range(blocks):
            pieces = [
                x_ref[b * PACK : (b + 1) * PACK, j * WIDTH : (j + 1) * WIDTH]
                for j in range(CHUNKS)
            ]
            out_ref[b * side : (b + 1) * side, :] = jnp.dot(
                pack, jnp.concatenate(pieces, axis=0), preferred_element_type=jnp.float32
            ).astype(jnp.bfloat16)


def run_expert(received, orders, weights, items):
    total = items * CHUNKS
    hidden_units = weights.shape[2]
    once = lambda a: pl.BlockSpec(a.shape, lambda f: (0, 0), pipeline_mode=pl.Buffered(1))
    return pl.pallas_call(
        expert_kernel,
        out_shape=jax.ShapeDtypeStruct((total, WIDTH), jnp.bfloat16),
        grid=(hidden_units // FF_BLOCK,),
        in_specs=[
            *(once(a) for a in (*received, *orders)),
            pl.BlockSpec((1, D, FF_BLOCK), lambda f: (0, 0, f)),
            pl.BlockSpec((1, D, FF_BLOCK), lambda f: (1, 0, f)),
            pl.BlockSpec((1, D, FF_BLOCK), lambda f: (2, 0, f)),
        ],
        out_specs=pl.BlockSpec((total, WIDTH), lambda f: (0, 0), pipeline_mode=pl.Buffered(1)),
        scratch_shapes=[
            pltpu.VMEM((items, D), jnp.bfloat16),
            pltpu.VMEM((items, D), jnp.float32),
        ],
        compiler_params=pltpu.CompilerParams(vmem_limit_bytes=36 * MIB),
        name="run_expert",
    )(*received, *orders, weights, weights, weights)


def combine_kernel(combine_ref, rows_ref, residual_ref, out_ref):
    combine = combine_ref[...]
    which = lax.broadcasted_iota(jnp.int32, combine.shape, 1) % CHUNKS
    left = jnp.concatenate(
        [jnp.where(which == j, combine, jnp.zeros_like(combine)) for j in range(CHUNKS)], axis=0
    )
    got = jnp.dot(left, rows_ref[...], preferred_element_type=jnp.float32)
    tokens = combine.shape[0]
    for j in range(CHUNKS):
        cols = slice(j * WIDTH, (j + 1) * WIDTH)
        out_ref[:, cols] = (
            residual_ref[:, cols].astype(jnp.float32) + got[j * tokens : (j + 1) * tokens, :]
        ).astype(out_ref.dtype)


def combine_rows(combine, rows, residual, dtype):
    return pl.pallas_call(
        combine_kernel,
        out_shape=jax.ShapeDtypeStruct(residual.shape, dtype),
        in_specs=[whole_vmem(), whole_vmem(), whole_vmem()],
        out_specs=whole_vmem(),
        compiler_params=pltpu.CompilerParams(vmem_limit_bytes=32 * MIB),
        name="combine_rows",
    )(combine, rows, residual)


def body(
    hidden,
    queries,
    latent,
    group_order,
    w_uk,
    w_uv,
    w_out,
    norm_gain,
    expert_ids,
    gate_weights,
    w_gate,
    w_up,
    w_down,
):
    ring, columns = lax.axis_size("z"), lax.axis_size("x")
    peers = columns * ring
    block_rows = hidden.shape[1]
    half_rows = block_rows // 2
    seq_rows = block_rows * lax.axis_size("ctx")
    whole = gather_directly(latent[0], "ctx")
    weights = [
        lax.all_gather(
            jnp.stack([w_gate[k], w_up[k], w_down[k]]), "ctx", axis=2, tiled=True
        )
        for k in range(LOCAL)
    ]
    row_index = jnp.arange(seq_rows, dtype=jnp.int32)
    positions = group_order[row_index // half_rows] * half_rows + row_index % half_rows
    own_positions = lax.dynamic_slice_in_dim(
        positions, lax.axis_index("ctx") * block_rows, block_rows
    )
    rank_of, gate_of = routing(expert_ids[0], gate_weights[0])
    combines = [combine_weights(rank_of, gate_of, k, peers) for k in range(LOCAL)]
    counts = (2 * NEAR + 1, ring - 2 * NEAR - 1)
    plans = [pick_plan(count, ring, columns) for count in counts]
    orders = [
        [unpick_matrix(first, count, k, ring) for first, count in zip((0, counts[0]), counts)]
        for k in range(LOCAL)
    ]
    table = jnp.pad(rank_of, ((0, 0), (0, EXTRA - EXPERTS)))

    content = whole[:, :KVR]
    key_rope = whole[:, KVR:]
    key_nope = jnp.dot(content, w_uk, preferred_element_type=jnp.float32).astype(jnp.bfloat16)
    values = jnp.dot(content, w_uv, preferred_element_type=jnp.float32).astype(jnp.bfloat16)
    query_full = queries[0].reshape(block_rows, HEADS, NOPE + ROPE)
    scores = jnp.einsum(
        "qhd,khd->hqk",
        query_full[:, :, :NOPE],
        key_nope.reshape(seq_rows, HEADS, NOPE),
        preferred_element_type=jnp.float32,
    )
    scores = scores + jnp.einsum(
        "qhr,kr->hqk", query_full[:, :, NOPE:], key_rope, preferred_element_type=jnp.float32
    )
    scores = scores * (NOPE + ROPE) ** (-0.5)
    visible = positions[None, :] <= own_positions[:, None]
    scores = jnp.where(visible[None], scores, -jnp.inf)
    peak = jnp.max(scores, axis=2, keepdims=True)
    expo = jnp.exp(scores - peak)
    totals = jnp.sum(expo, axis=2)
    heads_out = jnp.einsum(
        "hqk,khv->qhv",
        expo.astype(jnp.bfloat16),
        values.reshape(seq_rows, HEADS, VDIM),
        preferred_element_type=jnp.float32,
    )
    heads_out = heads_out / jnp.transpose(totals)[:, :, None]
    attended = heads_out.astype(jnp.bfloat16).reshape(block_rows, HEADS * VDIM)
    residual = (
        hidden[0].astype(jnp.float32) + jnp.dot(attended, w_out, preferred_element_type=jnp.float32)
    ).astype(jnp.bfloat16)
    stream = residual.astype(jnp.float32)
    factor = lax.rsqrt(jnp.mean(stream * stream, axis=1, keepdims=True) + EPSILON)
    normed = (stream * factor * norm_gain).astype(jnp.bfloat16)

    own = jnp.concatenate([normed, table], axis=1)
    up, down = [own], [own]
    for _ in range(NEAR + 1):
        up.append(shifted(up[-1], "z", 1))
        down.append(shifted(down[-1], "z", -1))
    half = block_rows // 2
    across = jnp.concatenate(
        [shifted(up[3][:half], "z", 1), shifted(down[3][half:], "z", -1)], axis=0
    )
    groups = ([up[2], up[1], own, down[1], down[2]], [down[3], across, up[3]])
    received = []
    for plan, blocks in zip(plans, groups):
        picked = pick_rows(plan, blocks).reshape(columns, -1, D)
        got = lax.all_to_all(picked, "x", split_axis=0, concat_axis=0, tiled=True)
        received.append(got.reshape(-1, D))
    items = peers * CAP
    returned = [
        exchanged(run_expert(received, orders[k], weights[k], items), peers) for k in range(LOCAL)
    ]
    mixed = residual
    for k in range(LOCAL):
        last = k == LOCAL - 1
        mixed = combine_rows(combines[k], returned[k], mixed, jnp.bfloat16 if last else jnp.float32)
    return mixed[None]


def solution(mesh):
    ctx, exp = mesh.devices.shape
    ring = 8
    mesh = Mesh(mesh.devices.reshape(ctx, exp // ring, ring), ("ctx", "x", "z"))
    part = P(("x", "z"), "ctx", None)
    units = P(("x", "z"), None, "ctx")
    return jax.shard_map(
        body,
        mesh=mesh,
        in_specs=(part, part, part, P(), P(), P(), P(), P(), part, part, units, units, units),
        out_specs=part,
        check_vma=False,
    )
```

```python
import jax
import jax.numpy as jnp
from jax import lax
from jax.experimental import pallas as pl
from jax.experimental.pallas import tpu as pltpu
from jax.sharding import Mesh
from jax.sharding import PartitionSpec as P

D = 2048
HEADS = 8
NOPE = 128
ROPE = 64
VDIM = 128
KVR = 512
EXPERTS = 64
TOPK = 6
CAP = 13
EPSILON = 1e-06

CHUNKS = 8
WIDTH = D // CHUNKS
LOCAL = 2
BLOCK = CAP * CHUNKS
PACK = 16
FF_BLOCK = 256
MIB = 1 << 20

EXTRA = 128
NEAR = 2


def gather_latent(own):
    near = [own, shifted(own, "y", 1), shifted(own, "y", -1), shifted(own, "y", 2)]
    mine = jnp.concatenate(near, axis=0)
    whole = jnp.concatenate([mine, shifted(mine, "core", 1)], axis=0)
    length, cores = lax.axis_size("y"), lax.axis_size("core")
    along = (lax.axis_index("y") + jnp.array([0, -1, 1, -2], jnp.int32)) % length
    core = lax.axis_index("core")
    places = [along * cores + (core + i) % cores for i in range(cores)]
    return whole, jnp.concatenate(places)


def exchanged(rows, peers):
    return lax.all_to_all(
        rows.reshape(peers, BLOCK, WIDTH), ("x", "z"), split_axis=0, concat_axis=0, tiled=True
    ).reshape(peers * BLOCK, WIDTH)


def routing(ids, gates):
    rows = ids.shape[0]
    chosen = ids[:, :, None] == jnp.arange(EXPERTS, dtype=jnp.int32)[None, None, :]
    named = jnp.any(chosen, axis=1)
    gate_of = jnp.sum(jnp.where(chosen, gates[:, :, None], 0.0), axis=1)
    order = jnp.arange(rows, dtype=jnp.int32)
    earlier = (order[None, :] < order[:, None]).astype(jnp.bfloat16)
    before = jnp.dot(earlier, named.astype(jnp.bfloat16), preferred_element_type=jnp.float32)
    rank_of = jnp.where(named, before, -1.0).astype(jnp.bfloat16)
    return rank_of, gate_of


def combine_weights(rank_of, gate_of, local, peers):
    total = peers * BLOCK
    row = jnp.arange(total, dtype=jnp.int32)
    expert = (row // BLOCK) * LOCAL + local
    rank = ((row % BLOCK) // CHUNKS).astype(jnp.float32)
    onehot = (expert[:, None] == jnp.arange(EXPERTS, dtype=jnp.int32)[None, :]).astype(jnp.bfloat16)
    at_cols = lax.dot_general(
        rank_of, onehot, (((1,), (1,)), ((), ())), preferred_element_type=jnp.float32
    )
    gate_cols = lax.dot_general(
        gate_of.astype(jnp.bfloat16),
        onehot,
        (((1,), (1,)), ((), ())),
        preferred_element_type=jnp.float32,
    )
    return jnp.where(at_cols == rank[None, :], gate_cols, 0.0).astype(jnp.bfloat16)


def shifted(rows, axis, by):
    length = lax.axis_size(axis)
    return lax.ppermute(rows, axis, [(i, (i + by) % length) for i in range(length)])


def group_rows(count):
    return -(-count * CAP // 8) * 8


def pick_plan(count, locals_, ring, columns):
    rows = group_rows(count * len(locals_))
    row = jnp.arange(rows, dtype=jnp.int32)
    local = row // (count * CAP)
    block = (row // CAP) % count
    rank = row % CAP
    target = jnp.arange(columns, dtype=jnp.int32)
    first = (target * ring + lax.axis_index("z")) * LOCAL + locals_[0]
    expert = (first[:, None] + local[None, :]).reshape(-1)
    onehot = expert[:, None] == jnp.arange(EXTRA, dtype=jnp.int32)[None, :]
    code = jnp.where(local < len(locals_), block * PACK + rank, -PACK).astype(jnp.float32)
    code = jnp.broadcast_to(jnp.tile(code, columns)[:, None], (columns * rows, EXTRA))
    return onehot.astype(jnp.bfloat16), code


def pick_kernel(onehot_ref, code_ref, *refs):
    blocks, (out_ref, made_ref, sems) = refs[:-3], refs[-3:]
    onehot, code = onehot_ref[...], code_ref[...]
    left = []
    for p, ref in enumerate(blocks):
        at = lax.dot_general(
            onehot, ref[:, D:], (((1,), (1,)), ((), ())), preferred_element_type=jnp.float32
        )
        left.append((at + float(p * PACK) == code).astype(jnp.float32).astype(jnp.bfloat16))
    left = jnp.concatenate(left, axis=1)
    copies = []
    for c in range(made_ref.shape[0]):
        width = made_ref.shape[2]
        cols = slice(c * width, (c + 1) * width)
        right = jnp.concatenate([ref[:, cols] for ref in blocks], axis=0)
        made_ref[c] = jnp.dot(left, right, preferred_element_type=jnp.float32).astype(jnp.bfloat16)
        copy = pltpu.make_async_copy(made_ref.at[c], out_ref.at[:, cols], sems.at[c])
        copy.start()
        copies.append(copy)
    for copy in copies:
        copy.wait()


def pick_rows(plan, blocks):
    total, width = plan[0].shape[0], 512
    return pl.pallas_call(
        pick_kernel,
        out_shape=jax.ShapeDtypeStruct((total, D), jnp.bfloat16),
        out_specs=pl.BlockSpec(memory_space=pltpu.HBM),
        scratch_shapes=[
            pltpu.VMEM((D // width, total, width), jnp.bfloat16),
            pltpu.SemaphoreType.DMA((D // width,)),
        ],
        compiler_params=pltpu.CompilerParams(vmem_limit_bytes=24 * MIB),
        name="pick_rows",
    )(*plan, *blocks)


def unpick_matrix(first, count, rows, offset, ring):
    out = jnp.arange(2 * ring * CAP, dtype=jnp.int32)
    source = (out // CAP) % ring
    listed = (source - lax.axis_index("z") + NEAR) % ring - first
    inside = (listed >= 0) & (listed < count)
    at = (out // (ring * CAP)) * rows + offset + listed * CAP + out % CAP
    col = jnp.arange(2 * rows, dtype=jnp.int32)
    return (inside[:, None] & (at[:, None] == col[None, :])).astype(jnp.bfloat16)


def pack_matrix():
    side = PACK * CHUNKS
    a = lax.broadcasted_iota(jnp.int32, (side, side), 1)
    b = lax.broadcasted_iota(jnp.int32, (side, side), 0)
    return (b == (a % PACK) * CHUNKS + a // PACK).astype(jnp.float32).astype(jnp.bfloat16)


def expert_kernel(
    near_ref, far_ref, near_order_ref, far_order_ref, gate_ref, up_ref, down_ref, out_ref, x_ref, acc_ref
):
    part = pl.program_id(0)
    parts = pl.num_programs(0)
    side = PACK * CHUNKS
    blocks = out_ref.shape[0] // side

    @pl.when(part == 0)
    def _():
        rows, near = near_order_ref.shape
        far = far_order_ref.shape[1]
        for i in range(x_ref.shape[0] // rows):
            got = jnp.dot(
                near_order_ref[...],
                near_ref[i * near : (i + 1) * near, :],
                preferred_element_type=jnp.float32,
            ) + jnp.dot(
                far_order_ref[...],
                far_ref[i * far : (i + 1) * far, :],
                preferred_element_type=jnp.float32,
            )
            x_ref[i * rows : (i + 1) * rows, :] = got.astype(jnp.bfloat16)

    x = x_ref[...]
    gate = jnp.dot(x, gate_ref[0], preferred_element_type=jnp.float32)
    up = jnp.dot(x, up_ref[0], preferred_element_type=jnp.float32)
    inner = (gate / (1.0 + jnp.exp(-gate)) * up).astype(jnp.bfloat16)
    out = lax.dot_general(
        inner, down_ref[0], (((1,), (1,)), ((), ())), preferred_element_type=jnp.float32
    )

    @pl.when(part == 0)
    def _():
        acc_ref[...] = out

    @pl.when((part > 0) & (part < parts - 1))
    def _():
        acc_ref[...] += out

    @pl.when(part == parts - 1)
    def _():
        x_ref[...] = (acc_ref[...] + out).astype(jnp.bfloat16)
        pack = pack_matrix()
        for b in range(blocks):
            pieces = [
                x_ref[b * PACK : (b + 1) * PACK, j * WIDTH : (j + 1) * WIDTH]
                for j in range(CHUNKS)
            ]
            out_ref[b * side : (b + 1) * side, :] = jnp.dot(
                pack, jnp.concatenate(pieces, axis=0), preferred_element_type=jnp.float32
            ).astype(jnp.bfloat16)


def run_expert(received, orders, weights, items):
    total = items * CHUNKS
    hidden_units = weights.shape[2]
    once = lambda a: pl.BlockSpec(a.shape, lambda f: (0, 0), pipeline_mode=pl.Buffered(1))
    return pl.pallas_call(
        expert_kernel,
        out_shape=jax.ShapeDtypeStruct((total, WIDTH), jnp.bfloat16),
        grid=(hidden_units // FF_BLOCK,),
        in_specs=[
            *(once(a) for a in (*received, *orders)),
            pl.BlockSpec((1, D, FF_BLOCK), lambda f: (0, 0, f)),
            pl.BlockSpec((1, D, FF_BLOCK), lambda f: (1, 0, f)),
            pl.BlockSpec((1, D, FF_BLOCK), lambda f: (2, 0, f)),
        ],
        out_specs=pl.BlockSpec((total, WIDTH), lambda f: (0, 0), pipeline_mode=pl.Buffered(1)),
        scratch_shapes=[
            pltpu.VMEM((items, D), jnp.bfloat16),
            pltpu.VMEM((items, D), jnp.float32),
        ],
        compiler_params=pltpu.CompilerParams(vmem_limit_bytes=54 * MIB),
        name="run_expert",
    )(*received, *orders, weights, weights, weights)


def combine_kernel(combine_hbm, rows_ref, base_hbm, out_ref, combine_ref, base_ref, sems):
    copies = [
        pltpu.make_async_copy(combine_hbm, combine_ref, sems.at[0]),
        pltpu.make_async_copy(base_hbm, base_ref, sems.at[1]),
    ]
    for copy in copies:
        copy.start()
    copies[0].wait()
    combine = combine_ref[...]
    which = lax.broadcasted_iota(jnp.int32, combine.shape, 1) % CHUNKS
    left = jnp.concatenate(
        [jnp.where(which == j, combine, jnp.zeros_like(combine)) for j in range(CHUNKS)], axis=0
    )
    got = jnp.dot(left, rows_ref[...], preferred_element_type=jnp.float32)
    copies[1].wait()
    tokens = combine.shape[0]
    for j in range(CHUNKS):
        cols = slice(j * WIDTH, (j + 1) * WIDTH)
        out_ref[:, cols] = (
            base_ref[:, cols].astype(jnp.float32) + got[j * tokens : (j + 1) * tokens, :]
        ).astype(out_ref.dtype)


def combine_rows(combine, rows, base, dtype):
    hbm, vmem = pl.BlockSpec(memory_space=pltpu.HBM), pl.BlockSpec(memory_space=pltpu.VMEM)
    return pl.pallas_call(
        combine_kernel,
        out_shape=jax.ShapeDtypeStruct(base.shape, dtype),
        in_specs=[hbm, vmem, hbm],
        scratch_shapes=[
            pltpu.VMEM(combine.shape, combine.dtype),
            pltpu.VMEM(base.shape, base.dtype),
            pltpu.SemaphoreType.DMA((2,)),
        ],
        compiler_params=pltpu.CompilerParams(vmem_limit_bytes=32 * MIB),
        name="combine_rows",
    )(combine, rows, base)


def body(
    hidden,
    queries,
    latent,
    group_order,
    w_uk,
    w_uv,
    w_out,
    norm_gain,
    expert_ids,
    gate_weights,
    w_gate,
    w_up,
    w_down,
):
    ring, columns = lax.axis_size("z"), lax.axis_size("x")
    peers = columns * ring
    block_rows = hidden.shape[1]
    half_rows = block_rows // 2
    whole, places = gather_latent(latent[0])
    seq_rows = whole.shape[0]
    inside = jnp.arange(half_rows, dtype=jnp.int32)

    def positions_of(blocks):
        halves = (blocks[:, None] * 2 + jnp.arange(2, dtype=jnp.int32)[None, :]).reshape(-1)
        return (group_order[halves][:, None] * half_rows + inside[None, :]).reshape(-1)

    positions = positions_of(places)
    own_positions = positions_of(places[:1])
    rank_of, gate_of = routing(expert_ids[0], gate_weights[0])
    combines = [combine_weights(rank_of, gate_of, k, peers) for k in range(LOCAL)]
    near_count, far_count = 2 * NEAR + 1, ring - 2 * NEAR - 1
    near_plan = pick_plan(near_count, range(LOCAL), ring, columns)
    far_plans = [pick_plan(far_count, [k], ring, columns) for k in range(LOCAL)]
    near_rows, far_rows = group_rows(near_count * LOCAL), group_rows(far_count)
    near_orders = [
        unpick_matrix(0, near_count, near_rows, k * near_count * CAP, ring) for k in range(LOCAL)
    ]
    far_order = unpick_matrix(near_count, far_count, far_rows, 0, ring)
    table = jnp.pad(rank_of, ((0, 0), (0, EXTRA - EXPERTS)))
    content = whole[:, :KVR]
    key_rope = whole[:, KVR:]
    key_nope = jnp.dot(content, w_uk, preferred_element_type=jnp.float32).astype(jnp.bfloat16)
    values = jnp.dot(content, w_uv, preferred_element_type=jnp.float32).astype(jnp.bfloat16)
    query_full = queries[0].reshape(block_rows, HEADS, NOPE + ROPE)
    scores = jnp.einsum(
        "qhd,khd->hqk",
        query_full[:, :, :NOPE],
        key_nope.reshape(seq_rows, HEADS, NOPE),
        preferred_element_type=jnp.float32,
    )
    scores = scores + jnp.einsum(
        "qhr,kr->hqk", query_full[:, :, NOPE:], key_rope, preferred_element_type=jnp.float32
    )
    scores = scores * (NOPE + ROPE) ** (-0.5)
    visible = positions[None, :] <= own_positions[:, None]
    scores = jnp.where(visible[None], scores, -jnp.inf)
    peak = jnp.max(scores, axis=2, keepdims=True)
    expo = jnp.exp(scores - peak)
    totals = jnp.sum(expo, axis=2)
    heads_out = jnp.einsum(
        "hqk,khv->qhv",
        expo.astype(jnp.bfloat16),
        values.reshape(seq_rows, HEADS, VDIM),
        preferred_element_type=jnp.float32,
    )
    heads_out = heads_out / jnp.transpose(totals)[:, :, None]
    attended = heads_out.astype(jnp.bfloat16).reshape(block_rows, HEADS * VDIM)
    residual = (
        hidden[0].astype(jnp.float32) + jnp.dot(attended, w_out, preferred_element_type=jnp.float32)
    ).astype(jnp.bfloat16)
    stream = residual.astype(jnp.float32)
    factor = lax.rsqrt(jnp.mean(stream * stream, axis=1, keepdims=True) + EPSILON)
    normed = (stream * factor * norm_gain).astype(jnp.bfloat16)

    shares = (w_gate, w_up, w_down)
    weights = []
    for k in range(LOCAL):
        if k:
            shares, _ = lax.optimization_barrier((shares, normed))
        stack = jnp.concatenate([w[k : k + 1] for w in shares])
        weights.append(lax.all_gather(stack, ("y", "core"), axis=2, tiled=True))

    own = jnp.concatenate([normed, table], axis=1)
    up, down = [own], [own]
    for _ in range(NEAR):
        up.append(shifted(up[-1], "z", 1))
        down.append(shifted(down[-1], "z", -1))
    near = [up[2], up[1], own, down[1], down[2]]

    def along_x(picked):
        picked = picked.reshape(columns, -1, D)
        return lax.all_to_all(picked, "x", split_axis=0, concat_axis=0, tiled=True).reshape(-1, D)

    first = pick_rows(near_plan, near)
    first, upper, lower = lax.optimization_barrier((first, up[NEAR], down[NEAR]))
    upper, lower = shifted(upper, "z", 1), shifted(lower, "z", -1)
    half = block_rows // 2
    across = jnp.concatenate(
        [shifted(upper[:half], "z", 1), shifted(lower[half:], "z", -1)], axis=0
    )
    from_near = along_x(first)
    before, from_far = from_near, []
    for k in range(LOCAL):
        picked = pick_rows(far_plans[k], [lower, across, upper])
        picked, _ = lax.optimization_barrier((picked, before))
        before = along_x(picked)
        from_far.append(before)
    items = peers * CAP
    returned = [
        exchanged(
            run_expert(
                (from_near, from_far[k]), (near_orders[k], far_order), weights[k], items
            ),
            peers,
        )
        for k in range(LOCAL)
    ]
    mixed = residual
    for k in range(LOCAL):
        last = k == LOCAL - 1
        mixed = combine_rows(combines[k], returned[k], mixed, jnp.bfloat16 if last else jnp.float32)
    return mixed[None]


def solution(mesh):
    ctx, exp = mesh.devices.shape
    cores, ring = 2, 8
    mesh = Mesh(
        mesh.devices.reshape(ctx // cores, cores, exp // ring, ring), ("y", "core", "x", "z")
    )
    ctx, exp = ("y", "core"), ("x", "z")
    part, units = P(exp, ctx, None), P(exp, None, ctx)
    return jax.shard_map(
        body,
        mesh=mesh,
        in_specs=(part, part, part, P(), P(), P(), P(), P(), part, part, units, units, units),
        out_specs=part,
        check_vma=False,
    )
```

```python
import jax
import jax.numpy as jnp
from jax import lax
from jax.experimental import pallas as pl
from jax.experimental.pallas import tpu as pltpu
from jax.sharding import Mesh
from jax.sharding import PartitionSpec as P

D = 2048
HEADS = 8
NOPE = 128
ROPE = 64
VDIM = 128
KVR = 512
EXPERTS = 64
TOPK = 6
CAP = 13
EPSILON = 1e-06

CHUNKS = 8
WIDTH = D // CHUNKS
LOCAL = 2
BLOCK = CAP * CHUNKS
PACK = 16
FF_BLOCK = 256
MIB = 1 << 20

EXTRA = 128
NEAR = 2


def gather_latent(own):
    near = [own, shifted(own, "y", 1), shifted(own, "y", -1), shifted(own, "y", 2)]
    mine = jnp.concatenate(near, axis=0)
    whole = jnp.concatenate([mine, shifted(mine, "core", 1)], axis=0)
    length, cores = lax.axis_size("y"), lax.axis_size("core")
    along = (lax.axis_index("y") + jnp.array([0, -1, 1, -2], jnp.int32)) % length
    core = lax.axis_index("core")
    places = [along * cores + (core + i) % cores for i in range(cores)]
    return whole, jnp.concatenate(places)


def exchanged(rows, peers):
    return lax.all_to_all(
        rows.reshape(peers, BLOCK, WIDTH), ("x", "z"), split_axis=0, concat_axis=0, tiled=True
    ).reshape(peers * BLOCK, WIDTH)


def routing(ids, gates):
    rows = ids.shape[0]
    chosen = ids[:, :, None] == jnp.arange(EXPERTS, dtype=jnp.int32)[None, None, :]
    named = jnp.any(chosen, axis=1)
    gate_of = jnp.sum(jnp.where(chosen, gates[:, :, None], 0.0), axis=1)
    order = jnp.arange(rows, dtype=jnp.int32)
    earlier = (order[None, :] < order[:, None]).astype(jnp.bfloat16)
    before = jnp.dot(earlier, named.astype(jnp.bfloat16), preferred_element_type=jnp.float32)
    rank_of = jnp.where(named, before, -1.0).astype(jnp.bfloat16)
    return rank_of, gate_of


def combine_weights(rank_of, gate_of, local, peers):
    total = peers * BLOCK
    row = jnp.arange(total, dtype=jnp.int32)
    expert = (row // BLOCK) * LOCAL + local
    rank = ((row % BLOCK) // CHUNKS).astype(jnp.float32)
    onehot = (expert[:, None] == jnp.arange(EXPERTS, dtype=jnp.int32)[None, :]).astype(jnp.bfloat16)
    at_cols = lax.dot_general(
        rank_of, onehot, (((1,), (1,)), ((), ())), preferred_element_type=jnp.float32
    )
    gate_cols = lax.dot_general(
        gate_of.astype(jnp.bfloat16),
        onehot,
        (((1,), (1,)), ((), ())),
        preferred_element_type=jnp.float32,
    )
    return jnp.where(at_cols == rank[None, :], gate_cols, 0.0).astype(jnp.bfloat16)


def shifted(rows, axis, by):
    length = lax.axis_size(axis)
    return lax.ppermute(rows, axis, [(i, (i + by) % length) for i in range(length)])


def group_rows(count):
    return -(-count * CAP // 8) * 8


def pick_plan(count, locals_, ring, columns):
    rows = group_rows(count * len(locals_))
    row = jnp.arange(rows, dtype=jnp.int32)
    local = row // (count * CAP)
    block = (row // CAP) % count
    rank = row % CAP
    target = jnp.arange(columns, dtype=jnp.int32)
    first = (target * ring + lax.axis_index("z")) * LOCAL + locals_[0]
    expert = (first[:, None] + local[None, :]).reshape(-1)
    onehot = expert[:, None] == jnp.arange(EXTRA, dtype=jnp.int32)[None, :]
    code = jnp.where(local < len(locals_), block * PACK + rank, -PACK).astype(jnp.float32)
    code = jnp.broadcast_to(jnp.tile(code, columns)[:, None], (columns * rows, EXTRA))
    return onehot.astype(jnp.bfloat16), code


def pick_kernel(onehot_ref, code_ref, *refs):
    blocks, (out_ref, made_ref, sems) = refs[:-3], refs[-3:]
    onehot, code = onehot_ref[...], code_ref[...]
    left = []
    for p, ref in enumerate(blocks):
        at = lax.dot_general(
            onehot, ref[:, D:], (((1,), (1,)), ((), ())), preferred_element_type=jnp.float32
        )
        left.append((at + float(p * PACK) == code).astype(jnp.float32).astype(jnp.bfloat16))
    left = jnp.concatenate(left, axis=1)
    copies = []
    for c in range(made_ref.shape[0]):
        width = made_ref.shape[2]
        cols = slice(c * width, (c + 1) * width)
        right = jnp.concatenate([ref[:, cols] for ref in blocks], axis=0)
        made_ref[c] = jnp.dot(left, right, preferred_element_type=jnp.float32).astype(jnp.bfloat16)
        copy = pltpu.make_async_copy(made_ref.at[c], out_ref.at[:, cols], sems.at[c])
        copy.start()
        copies.append(copy)
    for copy in copies:
        copy.wait()


def pick_rows(plan, blocks):
    total, width = plan[0].shape[0], 512
    return pl.pallas_call(
        pick_kernel,
        out_shape=jax.ShapeDtypeStruct((total, D), jnp.bfloat16),
        out_specs=pl.BlockSpec(memory_space=pltpu.HBM),
        scratch_shapes=[
            pltpu.VMEM((D // width, total, width), jnp.bfloat16),
            pltpu.SemaphoreType.DMA((D // width,)),
        ],
        compiler_params=pltpu.CompilerParams(vmem_limit_bytes=24 * MIB),
        name="pick_rows",
    )(*plan, *blocks)


def unpick_matrix(first, count, rows, offset, ring):
    out = jnp.arange(2 * ring * CAP, dtype=jnp.int32)
    source = (out // CAP) % ring
    listed = (source - lax.axis_index("z") + NEAR) % ring - first
    inside = (listed >= 0) & (listed < count)
    at = (out // (ring * CAP)) * rows + offset + listed * CAP + out % CAP
    col = jnp.arange(2 * rows, dtype=jnp.int32)
    return (inside[:, None] & (at[:, None] == col[None, :])).astype(jnp.bfloat16)


def pack_matrix():
    side = PACK * CHUNKS
    a = lax.broadcasted_iota(jnp.int32, (side, side), 1)
    b = lax.broadcasted_iota(jnp.int32, (side, side), 0)
    return (b == (a % PACK) * CHUNKS + a // PACK).astype(jnp.float32).astype(jnp.bfloat16)


def expert_kernel(
    near_ref, far_ref, near_order_ref, far_order_ref, gate_ref, up_ref, down_ref, out_ref, x_ref, acc_ref
):
    part = pl.program_id(0)
    parts = pl.num_programs(0)
    side = PACK * CHUNKS
    blocks = out_ref.shape[0] // side

    @pl.when(part == 0)
    def _():
        rows, near = near_order_ref.shape
        far = far_order_ref.shape[1]
        for i in range(x_ref.shape[0] // rows):
            got = jnp.dot(
                near_order_ref[...],
                near_ref[i * near : (i + 1) * near, :],
                preferred_element_type=jnp.float32,
            ) + jnp.dot(
                far_order_ref[...],
                far_ref[i * far : (i + 1) * far, :],
                preferred_element_type=jnp.float32,
            )
            x_ref[i * rows : (i + 1) * rows, :] = got.astype(jnp.bfloat16)

    x = x_ref[...]
    joined = lambda ref: jnp.concatenate([ref[i, 0] for i in range(ref.shape[0])], axis=1)
    gate = jnp.dot(x, joined(gate_ref), preferred_element_type=jnp.float32)
    up = jnp.dot(x, joined(up_ref), preferred_element_type=jnp.float32)
    inner = (gate / (1.0 + jnp.exp(-gate)) * up).astype(jnp.bfloat16)
    out = lax.dot_general(
        inner, joined(down_ref), (((1,), (1,)), ((), ())), preferred_element_type=jnp.float32
    )

    @pl.when(part == 0)
    def _():
        acc_ref[...] = out

    @pl.when((part > 0) & (part < parts - 1))
    def _():
        acc_ref[...] += out

    @pl.when(part == parts - 1)
    def _():
        x_ref[...] = (acc_ref[...] + out).astype(jnp.bfloat16)
        pack = pack_matrix()
        for b in range(blocks):
            pieces = [
                x_ref[b * PACK : (b + 1) * PACK, j * WIDTH : (j + 1) * WIDTH]
                for j in range(CHUNKS)
            ]
            out_ref[b * side : (b + 1) * side, :] = jnp.dot(
                pack, jnp.concatenate(pieces, axis=0), preferred_element_type=jnp.float32
            ).astype(jnp.bfloat16)


def run_expert(received, orders, weights, items):
    total = items * CHUNKS
    shares, _, _, width = weights.shape
    step = FF_BLOCK // width
    once = lambda a: pl.BlockSpec(a.shape, lambda f: (0, 0), pipeline_mode=pl.Buffered(1))
    return pl.pallas_call(
        expert_kernel,
        out_shape=jax.ShapeDtypeStruct((total, WIDTH), jnp.bfloat16),
        grid=(shares // step,),
        in_specs=[
            *(once(a) for a in (*received, *orders)),
            pl.BlockSpec((step, 1, D, width), lambda f: (f, 0, 0, 0)),
            pl.BlockSpec((step, 1, D, width), lambda f: (f, 1, 0, 0)),
            pl.BlockSpec((step, 1, D, width), lambda f: (f, 2, 0, 0)),
        ],
        out_specs=pl.BlockSpec((total, WIDTH), lambda f: (0, 0), pipeline_mode=pl.Buffered(1)),
        scratch_shapes=[
            pltpu.VMEM((items, D), jnp.bfloat16),
            pltpu.VMEM((items, D), jnp.float32),
        ],
        compiler_params=pltpu.CompilerParams(vmem_limit_bytes=54 * MIB),
        name="run_expert",
    )(*received, *orders, weights, weights, weights)


def combine_kernel(combine_ref, rows_ref, base_ref, out_ref):
    combine = combine_ref[...]
    which = lax.broadcasted_iota(jnp.int32, combine.shape, 1) % CHUNKS
    left = jnp.concatenate(
        [jnp.where(which == j, combine, jnp.zeros_like(combine)) for j in range(CHUNKS)], axis=0
    )
    got = jnp.dot(left, rows_ref[...], preferred_element_type=jnp.float32)
    tokens = combine.shape[0]
    for j in range(CHUNKS):
        cols = slice(j * WIDTH, (j + 1) * WIDTH)
        out_ref[:, cols] = (
            base_ref[:, cols].astype(jnp.float32) + got[j * tokens : (j + 1) * tokens, :]
        ).astype(out_ref.dtype)


def combine_rows(combine, rows, base, dtype):
    whole = lambda a: pl.BlockSpec(a.shape, lambda i: (0, 0), pipeline_mode=pl.Buffered(1))
    return pl.pallas_call(
        combine_kernel,
        out_shape=jax.ShapeDtypeStruct(base.shape, dtype),
        grid=(1,),
        in_specs=[whole(combine), whole(rows), whole(base)],
        out_specs=whole(base),
        compiler_params=pltpu.CompilerParams(vmem_limit_bytes=58 * MIB),
        name="combine_rows",
    )(combine, rows, base)


def body(
    hidden,
    queries,
    latent,
    group_order,
    w_uk,
    w_uv,
    w_out,
    norm_gain,
    expert_ids,
    gate_weights,
    w_gate,
    w_up,
    w_down,
):
    ring, columns = lax.axis_size("z"), lax.axis_size("x")
    peers = columns * ring
    block_rows = hidden.shape[1]
    half_rows = block_rows // 2
    whole, places = gather_latent(latent[0])
    weights = []
    for k in range(LOCAL):
        stack = jnp.concatenate([w[k : k + 1] for w in (w_gate, w_up, w_down)])
        weights.append(lax.all_gather(stack, ("y", "core"), axis=0))
    seq_rows = whole.shape[0]
    inside = jnp.arange(half_rows, dtype=jnp.int32)

    def positions_of(blocks):
        halves = (blocks[:, None] * 2 + jnp.arange(2, dtype=jnp.int32)[None, :]).reshape(-1)
        return (group_order[halves][:, None] * half_rows + inside[None, :]).reshape(-1)

    positions = positions_of(places)
    own_positions = positions_of(places[:1])
    rank_of, gate_of = routing(expert_ids[0], gate_weights[0])
    combines = [combine_weights(rank_of, gate_of, k, peers) for k in range(LOCAL)]
    near_count, far_count = 2 * NEAR + 1, ring - 2 * NEAR - 1
    near_plan = pick_plan(near_count, range(LOCAL), ring, columns)
    far_plans = [pick_plan(far_count, [k], ring, columns) for k in range(LOCAL)]
    near_rows, far_rows = group_rows(near_count * LOCAL), group_rows(far_count)
    near_orders = [
        unpick_matrix(0, near_count, near_rows, k * near_count * CAP, ring) for k in range(LOCAL)
    ]
    far_order = unpick_matrix(near_count, far_count, far_rows, 0, ring)
    table = jnp.pad(rank_of, ((0, 0), (0, EXTRA - EXPERTS)))
    content = whole[:, :KVR]
    key_rope = whole[:, KVR:]
    key_nope = jnp.dot(content, w_uk, preferred_element_type=jnp.float32).astype(jnp.bfloat16)
    values = jnp.dot(content, w_uv, preferred_element_type=jnp.float32).astype(jnp.bfloat16)
    query_full = queries[0].reshape(block_rows, HEADS, NOPE + ROPE)
    scores = jnp.einsum(
        "qhd,khd->hqk",
        query_full[:, :, :NOPE],
        key_nope.reshape(seq_rows, HEADS, NOPE),
        preferred_element_type=jnp.float32,
    )
    scores = scores + jnp.einsum(
        "qhr,kr->hqk", query_full[:, :, NOPE:], key_rope, preferred_element_type=jnp.float32
    )
    scores = scores * (NOPE + ROPE) ** (-0.5)
    visible = positions[None, :] <= own_positions[:, None]
    scores = jnp.where(visible[None], scores, -jnp.inf)
    peak = jnp.max(scores, axis=2, keepdims=True)
    expo = jnp.exp(scores - peak)
    totals = jnp.sum(expo, axis=2)
    heads_out = jnp.einsum(
        "hqk,khv->qhv",
        expo.astype(jnp.bfloat16),
        values.reshape(seq_rows, HEADS, VDIM),
        preferred_element_type=jnp.float32,
    )
    heads_out = heads_out / jnp.transpose(totals)[:, :, None]
    attended = heads_out.astype(jnp.bfloat16).reshape(block_rows, HEADS * VDIM)
    residual = (
        hidden[0].astype(jnp.float32) + jnp.dot(attended, w_out, preferred_element_type=jnp.float32)
    ).astype(jnp.bfloat16)
    stream = residual.astype(jnp.float32)
    factor = lax.rsqrt(jnp.mean(stream * stream, axis=1, keepdims=True) + EPSILON)
    normed = (stream * factor * norm_gain).astype(jnp.bfloat16)

    own = jnp.concatenate([normed, table], axis=1)
    up, down = [own], [own]
    for _ in range(NEAR):
        up.append(shifted(up[-1], "z", 1))
        down.append(shifted(down[-1], "z", -1))
    near = [up[2], up[1], own, down[1], down[2]]

    def along_x(picked):
        picked = picked.reshape(columns, -1, D)
        return lax.all_to_all(picked, "x", split_axis=0, concat_axis=0, tiled=True).reshape(-1, D)

    first = pick_rows(near_plan, near)
    first, upper, lower = lax.optimization_barrier((first, up[NEAR], down[NEAR]))
    upper, lower = shifted(upper, "z", 1), shifted(lower, "z", -1)
    half = block_rows // 2
    across = jnp.concatenate(
        [shifted(upper[:half], "z", 1), shifted(lower[half:], "z", -1)], axis=0
    )
    from_near = along_x(first)
    before, from_far = from_near, []
    for k in range(LOCAL):
        picked = pick_rows(far_plans[k], [lower, across, upper])
        picked, _ = lax.optimization_barrier((picked, before))
        before = along_x(picked)
        from_far.append(before)
    items = peers * CAP
    returned = [
        exchanged(
            run_expert(
                (from_near, from_far[k]), (near_orders[k], far_order), weights[k], items
            ),
            peers,
        )
        for k in range(LOCAL)
    ]
    mixed = residual
    for k in range(LOCAL):
        last = k == LOCAL - 1
        mixed = combine_rows(combines[k], returned[k], mixed, jnp.bfloat16 if last else jnp.float32)
    return mixed[None]


def solution(mesh):
    ctx, exp = mesh.devices.shape
    cores, ring = 2, 8
    mesh = Mesh(
        mesh.devices.reshape(ctx // cores, cores, exp // ring, ring), ("y", "core", "x", "z")
    )
    ctx, exp = ("y", "core"), ("x", "z")
    part, units = P(exp, ctx, None), P(exp, None, ctx)
    return jax.shard_map(
        body,
        mesh=mesh,
        in_specs=(part, part, part, P(), P(), P(), P(), P(), part, part, units, units, units),
        out_specs=part,
        check_vma=False,
    )
```

```python
import jax
import jax.numpy as jnp
from jax import lax
from jax.experimental import pallas as pl
from jax.experimental.pallas import tpu as pltpu
from jax.sharding import Mesh
from jax.sharding import PartitionSpec as P

D = 2048
HEADS = 8
NOPE = 128
ROPE = 64
VDIM = 128
KVR = 512
EXPERTS = 64
TOPK = 6
CAP = 13
EPSILON = 1e-06

CHUNKS = 8
WIDTH = D // CHUNKS
LOCAL = 2
BLOCK = CAP * CHUNKS
PACK = 16
FF_BLOCK = 256
MIB = 1 << 20

EXTRA = 128
DISTANCES = ((-1, 0, 1), (-2, 2), (3, 4, -3))


def gather_latent(own):
    near = [own, shifted(own, "y", 1), shifted(own, "y", -1), shifted(own, "y", 2)]
    mine = jnp.concatenate(near, axis=0)
    whole = jnp.concatenate([mine, shifted(mine, "core", 1)], axis=0)
    length, cores = lax.axis_size("y"), lax.axis_size("core")
    along = (lax.axis_index("y") + jnp.array([0, -1, 1, -2], jnp.int32)) % length
    core = lax.axis_index("core")
    places = [along * cores + (core + i) % cores for i in range(cores)]
    return whole, jnp.concatenate(places)


def exchanged(rows, peers):
    return lax.all_to_all(
        rows.reshape(peers, BLOCK, WIDTH), ("x", "z"), split_axis=0, concat_axis=0, tiled=True
    ).reshape(peers * BLOCK, WIDTH)


def routing(ids, gates):
    rows = ids.shape[0]
    chosen = ids[:, :, None] == jnp.arange(EXPERTS, dtype=jnp.int32)[None, None, :]
    named = jnp.any(chosen, axis=1)
    gate_of = jnp.sum(jnp.where(chosen, gates[:, :, None], 0.0), axis=1)
    order = jnp.arange(rows, dtype=jnp.int32)
    earlier = (order[None, :] < order[:, None]).astype(jnp.bfloat16)
    before = jnp.dot(earlier, named.astype(jnp.bfloat16), preferred_element_type=jnp.float32)
    rank_of = jnp.where(named, before, -1.0).astype(jnp.bfloat16)
    return rank_of, gate_of


def combine_weights(rank_of, gate_of, local, peers):
    total = peers * BLOCK
    row = jnp.arange(total, dtype=jnp.int32)
    expert = (row // BLOCK) * LOCAL + local
    rank = ((row % BLOCK) // CHUNKS).astype(jnp.float32)
    onehot = (expert[:, None] == jnp.arange(EXPERTS, dtype=jnp.int32)[None, :]).astype(jnp.bfloat16)
    at_cols = lax.dot_general(
        rank_of, onehot, (((1,), (1,)), ((), ())), preferred_element_type=jnp.float32
    )
    gate_cols = lax.dot_general(
        gate_of.astype(jnp.bfloat16),
        onehot,
        (((1,), (1,)), ((), ())),
        preferred_element_type=jnp.float32,
    )
    return jnp.where(at_cols == rank[None, :], gate_cols, 0.0).astype(jnp.bfloat16)


def shifted(rows, axis, by):
    length = lax.axis_size(axis)
    return lax.ppermute(rows, axis, [(i, (i + by) % length) for i in range(length)])


def held(*arrays):
    return lax.optimization_barrier(arrays)


def group_rows(count):
    return -(-count * CAP // 8) * 8


def pick_plan(count, locals_, ring, columns):
    rows = group_rows(count * len(locals_))
    row = jnp.arange(rows, dtype=jnp.int32)
    local = row // (count * CAP)
    block = (row // CAP) % count
    rank = row % CAP
    target = jnp.arange(columns, dtype=jnp.int32)
    first = (target * ring + lax.axis_index("z")) * LOCAL + locals_[0]
    expert = (first[:, None] + local[None, :]).reshape(-1)
    onehot = expert[:, None] == jnp.arange(EXTRA, dtype=jnp.int32)[None, :]
    code = jnp.where(local < len(locals_), block * PACK + rank, -PACK).astype(jnp.float32)
    code = jnp.broadcast_to(jnp.tile(code, columns)[:, None], (columns * rows, EXTRA))
    return onehot.astype(jnp.bfloat16), code


def pick_kernel(onehot_ref, code_ref, *refs):
    blocks, (out_ref, made_ref, sems) = refs[:-3], refs[-3:]
    onehot, code = onehot_ref[...], code_ref[...]
    left = []
    for p, ref in enumerate(blocks):
        at = lax.dot_general(
            onehot, ref[:, D:], (((1,), (1,)), ((), ())), preferred_element_type=jnp.float32
        )
        left.append((at + float(p * PACK) == code).astype(jnp.float32).astype(jnp.bfloat16))
    left = jnp.concatenate(left, axis=1)
    copies = []
    for c in range(made_ref.shape[0]):
        width = made_ref.shape[2]
        cols = slice(c * width, (c + 1) * width)
        right = jnp.concatenate([ref[:, cols] for ref in blocks], axis=0)
        made_ref[c] = jnp.dot(left, right, preferred_element_type=jnp.float32).astype(jnp.bfloat16)
        copy = pltpu.make_async_copy(made_ref.at[c], out_ref.at[:, cols], sems.at[c])
        copy.start()
        copies.append(copy)
    for copy in copies:
        copy.wait()


def pick_rows(plan, blocks):
    total, width = plan[0].shape[0], 512
    return pl.pallas_call(
        pick_kernel,
        out_shape=jax.ShapeDtypeStruct((total, D), jnp.bfloat16),
        out_specs=pl.BlockSpec(memory_space=pltpu.HBM),
        scratch_shapes=[
            pltpu.VMEM((D // width, total, width), jnp.bfloat16),
            pltpu.SemaphoreType.DMA((D // width,)),
        ],
        compiler_params=pltpu.CompilerParams(vmem_limit_bytes=24 * MIB),
        name="pick_rows",
    )(*plan, *blocks)


def unpick_matrix(distances, rows, offset, ring):
    out = jnp.arange(2 * ring * CAP, dtype=jnp.int32)
    distance = ((out // CAP) % ring - lax.axis_index("z")) % ring
    inside, listed = jnp.zeros(out.shape, bool), jnp.zeros_like(out)
    for i, d in enumerate(distances):
        here = distance == d % ring
        inside, listed = inside | here, jnp.where(here, i, listed)
    at = (out // (ring * CAP)) * rows + offset + listed * CAP + out % CAP
    col = jnp.arange(2 * rows, dtype=jnp.int32)
    return (inside[:, None] & (at[:, None] == col[None, :])).astype(jnp.bfloat16)


def pack_matrix():
    side = PACK * CHUNKS
    a = lax.broadcasted_iota(jnp.int32, (side, side), 1)
    b = lax.broadcasted_iota(jnp.int32, (side, side), 0)
    return (b == (a % PACK) * CHUNKS + a // PACK).astype(jnp.float32).astype(jnp.bfloat16)


def expert_kernel(*refs):
    groups = len(DISTANCES)
    received, orders = refs[:groups], refs[groups : 2 * groups]
    gate_ref, up_ref, down_ref, out_ref, x_ref, acc_ref = refs[2 * groups :]
    part = pl.program_id(0)
    parts = pl.num_programs(0)
    side = PACK * CHUNKS
    blocks = out_ref.shape[0] // side

    @pl.when(part == 0)
    def _():
        rows = orders[0].shape[0]
        for i in range(x_ref.shape[0] // rows):
            got = 0.0
            for ref, order in zip(received, orders):
                cols = order.shape[1]
                got = got + jnp.dot(
                    order[...],
                    ref[i * cols : (i + 1) * cols, :],
                    preferred_element_type=jnp.float32,
                )
            x_ref[i * rows : (i + 1) * rows, :] = got.astype(jnp.bfloat16)

    x = x_ref[...]
    joined = lambda ref: jnp.concatenate([ref[i, 0] for i in range(ref.shape[0])], axis=1)
    gate = jnp.dot(x, joined(gate_ref), preferred_element_type=jnp.float32)
    up = jnp.dot(x, joined(up_ref), preferred_element_type=jnp.float32)
    inner = (gate / (1.0 + jnp.exp(-gate)) * up).astype(jnp.bfloat16)
    out = lax.dot_general(
        inner, joined(down_ref), (((1,), (1,)), ((), ())), preferred_element_type=jnp.float32
    )

    @pl.when(part == 0)
    def _():
        acc_ref[...] = out

    @pl.when((part > 0) & (part < parts - 1))
    def _():
        acc_ref[...] += out

    @pl.when(part == parts - 1)
    def _():
        x_ref[...] = (acc_ref[...] + out).astype(jnp.bfloat16)
        pack = pack_matrix()
        for b in range(blocks):
            pieces = [
                x_ref[b * PACK : (b + 1) * PACK, j * WIDTH : (j + 1) * WIDTH]
                for j in range(CHUNKS)
            ]
            out_ref[b * side : (b + 1) * side, :] = jnp.dot(
                pack, jnp.concatenate(pieces, axis=0), preferred_element_type=jnp.float32
            ).astype(jnp.bfloat16)


def run_expert(received, orders, weights, items):
    total = items * CHUNKS
    shares, _, _, width = weights.shape
    step = FF_BLOCK // width
    once = lambda a: pl.BlockSpec(a.shape, lambda f: (0, 0), pipeline_mode=pl.Buffered(1))
    return pl.pallas_call(
        expert_kernel,
        out_shape=jax.ShapeDtypeStruct((total, WIDTH), jnp.bfloat16),
        grid=(shares // step,),
        in_specs=[
            *(once(a) for a in (*received, *orders)),
            pl.BlockSpec((step, 1, D, width), lambda f: (f, 0, 0, 0)),
            pl.BlockSpec((step, 1, D, width), lambda f: (f, 1, 0, 0)),
            pl.BlockSpec((step, 1, D, width), lambda f: (f, 2, 0, 0)),
        ],
        out_specs=pl.BlockSpec((total, WIDTH), lambda f: (0, 0), pipeline_mode=pl.Buffered(1)),
        scratch_shapes=[
            pltpu.VMEM((items, D), jnp.bfloat16),
            pltpu.VMEM((items, D), jnp.float32),
        ],
        compiler_params=pltpu.CompilerParams(vmem_limit_bytes=54 * MIB),
        name="run_expert",
    )(*received, *orders, weights, weights, weights)


def combine_kernel(combine_ref, rows_ref, base_ref, out_ref):
    combine = combine_ref[...]
    which = lax.broadcasted_iota(jnp.int32, combine.shape, 1) % CHUNKS
    left = jnp.concatenate(
        [jnp.where(which == j, combine, jnp.zeros_like(combine)) for j in range(CHUNKS)], axis=0
    )
    got = jnp.dot(left, rows_ref[...], preferred_element_type=jnp.float32)
    tokens = combine.shape[0]
    for j in range(CHUNKS):
        cols = slice(j * WIDTH, (j + 1) * WIDTH)
        out_ref[:, cols] = (
            base_ref[:, cols].astype(jnp.float32) + got[j * tokens : (j + 1) * tokens, :]
        ).astype(out_ref.dtype)


def combine_rows(combine, rows, base, dtype):
    vmem = pl.BlockSpec(memory_space=pltpu.VMEM)
    return pl.pallas_call(
        combine_kernel,
        out_shape=jax.ShapeDtypeStruct(base.shape, dtype),
        in_specs=[vmem] * 3,
        out_specs=vmem,
        compiler_params=pltpu.CompilerParams(vmem_limit_bytes=32 * MIB),
        name="combine_rows",
    )(combine, rows, base)


def body(
    hidden,
    queries,
    latent,
    group_order,
    w_uk,
    w_uv,
    w_out,
    norm_gain,
    expert_ids,
    gate_weights,
    w_gate,
    w_up,
    w_down,
):
    ring, columns = lax.axis_size("z"), lax.axis_size("x")
    peers = columns * ring
    block_rows = hidden.shape[1]
    half_rows = block_rows // 2
    whole, places = gather_latent(latent[0])
    weights = []
    for k in range(LOCAL):
        stack = jnp.concatenate([w[k : k + 1] for w in (w_gate, w_up, w_down)])
        weights.append(lax.all_gather(stack, ("y", "core"), axis=0))
    seq_rows = whole.shape[0]
    inside = jnp.arange(half_rows, dtype=jnp.int32)

    def positions_of(blocks):
        halves = (blocks[:, None] * 2 + jnp.arange(2, dtype=jnp.int32)[None, :]).reshape(-1)
        return (group_order[halves][:, None] * half_rows + inside[None, :]).reshape(-1)

    positions = positions_of(places)
    own_positions = positions_of(places[:1])
    rank_of, gate_of = routing(expert_ids[0], gate_weights[0])
    combines = [combine_weights(rank_of, gate_of, k, peers) for k in range(LOCAL)]
    both, alone = range(LOCAL), [[k] for k in range(LOCAL)]
    plans, orders = [], [[] for _ in both]
    for distances in DISTANCES:
        count = len(distances)
        together = distances is not DISTANCES[-1]
        plans.append([pick_plan(count, g, ring, columns) for g in ([both] if together else alone)])
        rows = group_rows(count * (LOCAL if together else 1))
        for k in both:
            offset = k * count * CAP if together else 0
            orders[k].append(unpick_matrix(distances, rows, offset, ring))
    table = jnp.pad(rank_of, ((0, 0), (0, EXTRA - EXPERTS)))
    content = whole[:, :KVR]
    key_rope = whole[:, KVR:]
    key_nope = jnp.dot(content, w_uk, preferred_element_type=jnp.float32).astype(jnp.bfloat16)
    values = jnp.dot(content, w_uv, preferred_element_type=jnp.float32).astype(jnp.bfloat16)
    query_full = queries[0].reshape(block_rows, HEADS, NOPE + ROPE)
    scores = jnp.einsum(
        "qhd,khd->hqk",
        query_full[:, :, :NOPE],
        key_nope.reshape(seq_rows, HEADS, NOPE),
        preferred_element_type=jnp.float32,
    )
    scores = scores + jnp.einsum(
        "qhr,kr->hqk", query_full[:, :, NOPE:], key_rope, preferred_element_type=jnp.float32
    )
    scores = scores * (NOPE + ROPE) ** (-0.5)
    visible = positions[None, :] <= own_positions[:, None]
    scores = jnp.where(visible[None], scores, -jnp.inf)
    peak = jnp.max(scores, axis=2, keepdims=True)
    expo = jnp.exp(scores - peak)
    totals = jnp.sum(expo, axis=2)
    heads_out = jnp.einsum(
        "hqk,khv->qhv",
        expo.astype(jnp.bfloat16),
        values.reshape(seq_rows, HEADS, VDIM),
        preferred_element_type=jnp.float32,
    )
    heads_out = heads_out / jnp.transpose(totals)[:, :, None]
    attended = heads_out.astype(jnp.bfloat16).reshape(block_rows, HEADS * VDIM)
    residual = (
        hidden[0].astype(jnp.float32) + jnp.dot(attended, w_out, preferred_element_type=jnp.float32)
    ).astype(jnp.bfloat16)
    stream = residual.astype(jnp.float32)
    factor = lax.rsqrt(jnp.mean(stream * stream, axis=1, keepdims=True) + EPSILON)
    normed = (stream * factor * norm_gain).astype(jnp.bfloat16)

    own = jnp.concatenate([normed, table], axis=1)
    def along_x(picked):
        picked = picked.reshape(columns, -1, D)
        return lax.all_to_all(picked, "x", split_axis=0, concat_axis=0, tiled=True).reshape(-1, D)

    up1, down1 = shifted(own, "z", 1), shifted(own, "z", -1)
    up2, down2 = shifted(up1, "z", 1), shifted(down1, "z", -1)
    first = pick_rows(plans[0][0], [up1, own, down1])
    from_first = along_x(first)
    second = pick_rows(plans[1][0], [up2, down2])
    _, up2, down2 = held(first, up2, down2)
    up3, down3 = shifted(up2, "z", 1), shifted(down2, "z", -1)
    second, _ = held(second, from_first)
    from_second = along_x(second)
    half = block_rows // 2
    across = jnp.concatenate(
        [shifted(up3[:half], "z", 1), shifted(down3[half:], "z", -1)], axis=0
    )
    before, from_last = from_second, []
    for k in range(LOCAL):
        picked = pick_rows(plans[2][k], [down3, across, up3])
        picked, _ = held(picked, before)
        before = along_x(picked)
        from_last.append(before)
    items = peers * CAP
    returned = [
        exchanged(
            run_expert((from_first, from_second, from_last[k]), orders[k], weights[k], items),
            peers,
        )
        for k in range(LOCAL)
    ]
    mixed = residual
    for k in range(LOCAL):
        last = k == LOCAL - 1
        mixed = combine_rows(combines[k], returned[k], mixed, jnp.bfloat16 if last else jnp.float32)
    return mixed[None]


def solution(mesh):
    ctx, exp = mesh.devices.shape
    cores, ring = 2, 8
    mesh = Mesh(
        mesh.devices.reshape(ctx // cores, cores, exp // ring, ring), ("y", "core", "x", "z")
    )
    ctx, exp = ("y", "core"), ("x", "z")
    part, units = P(exp, ctx, None), P(exp, None, ctx)
    return jax.shard_map(
        body,
        mesh=mesh,
        in_specs=(part, part, part, P(), P(), P(), P(), P(), part, part, units, units, units),
        out_specs=part,
        check_vma=False,
    )
```

```python
import jax
import jax.numpy as jnp
from jax import lax
from jax.experimental import pallas as pl
from jax.experimental.pallas import tpu as pltpu
from jax.sharding import Mesh
from jax.sharding import PartitionSpec as P

D = 2048
HEADS = 8
NOPE = 128
ROPE = 64
VDIM = 128
KVR = 512
EXPERTS = 64
TOPK = 6
CAP = 13
EPSILON = 1e-06

CHUNKS = 8
WIDTH = D // CHUNKS
LOCAL = 2
BLOCK = CAP * CHUNKS
PACK = 16
FF_BLOCK = 256
MIB = 1 << 20

EXTRA = 128
DISTANCES = ((-1, 0, 1), (-2, 2), (3, 4, -3))


def gather_latent(own, ready):
    near = [own, shifted(own, "y", 1), shifted(own, "y", -1), shifted(own, "y", 2)]
    mine, ready = held(jnp.concatenate(near, axis=0), ready)
    whole = jnp.concatenate([mine, shifted(mine, "core", 1)], axis=0)
    length, cores = lax.axis_size("y"), lax.axis_size("core")
    along = (lax.axis_index("y") + jnp.array([0, -1, 1, -2], jnp.int32)) % length
    core = lax.axis_index("core")
    places = [along * cores + (core + i) % cores for i in range(cores)]
    return whole, jnp.concatenate(places), ready


def gather_weights(shares, local):
    stack = jnp.concatenate([w[local : local + 1] for w in shares])
    return lax.all_gather(stack, ("y", "core"), axis=0)


def exchanged(rows, peers):
    return lax.all_to_all(
        rows.reshape(peers, BLOCK, WIDTH), ("x", "z"), split_axis=0, concat_axis=0, tiled=True
    ).reshape(peers * BLOCK, WIDTH)


def routing(ids, gates):
    rows = ids.shape[0]
    chosen = ids[:, :, None] == jnp.arange(EXPERTS, dtype=jnp.int32)[None, None, :]
    named = jnp.any(chosen, axis=1)
    gate_of = jnp.sum(jnp.where(chosen, gates[:, :, None], 0.0), axis=1)
    order = jnp.arange(rows, dtype=jnp.int32)
    earlier = (order[None, :] < order[:, None]).astype(jnp.bfloat16)
    before = jnp.dot(earlier, named.astype(jnp.bfloat16), preferred_element_type=jnp.float32)
    rank_of = jnp.where(named, before, -1.0).astype(jnp.bfloat16)
    return rank_of, gate_of


def combine_weights(rank_of, gate_of, local, peers):
    total = peers * BLOCK
    row = jnp.arange(total, dtype=jnp.int32)
    expert = (row // BLOCK) * LOCAL + local
    rank = ((row % BLOCK) // CHUNKS).astype(jnp.float32)
    onehot = (expert[:, None] == jnp.arange(EXPERTS, dtype=jnp.int32)[None, :]).astype(jnp.bfloat16)
    at_cols = lax.dot_general(
        rank_of, onehot, (((1,), (1,)), ((), ())), preferred_element_type=jnp.float32
    )
    gate_cols = lax.dot_general(
        gate_of.astype(jnp.bfloat16),
        onehot,
        (((1,), (1,)), ((), ())),
        preferred_element_type=jnp.float32,
    )
    return jnp.where(at_cols == rank[None, :], gate_cols, 0.0).astype(jnp.bfloat16)


def shifted(rows, axis, by):
    length = lax.axis_size(axis)
    return lax.ppermute(rows, axis, [(i, (i + by) % length) for i in range(length)])


def held(*arrays):
    return lax.optimization_barrier(arrays)


def group_rows(count):
    return -(-count * CAP // 8) * 8


def pick_plan(count, locals_, ring, columns):
    rows = group_rows(count * len(locals_))
    row = jnp.arange(rows, dtype=jnp.int32)
    local = row // (count * CAP)
    block = (row // CAP) % count
    rank = row % CAP
    target = jnp.arange(columns, dtype=jnp.int32)
    first = (target * ring + lax.axis_index("z")) * LOCAL + locals_[0]
    expert = (first[:, None] + local[None, :]).reshape(-1)
    onehot = expert[:, None] == jnp.arange(EXTRA, dtype=jnp.int32)[None, :]
    code = jnp.where(local < len(locals_), block * PACK + rank, -PACK).astype(jnp.float32)
    code = jnp.broadcast_to(jnp.tile(code, columns)[:, None], (columns * rows, EXTRA))
    return onehot.astype(jnp.bfloat16), code


def pick_kernel(onehot_ref, code_ref, *refs):
    blocks, (out_ref, made_ref, sems) = refs[:-3], refs[-3:]
    onehot, code = onehot_ref[...], code_ref[...]
    left = []
    for p, ref in enumerate(blocks):
        at = lax.dot_general(
            onehot, ref[:, D:], (((1,), (1,)), ((), ())), preferred_element_type=jnp.float32
        )
        left.append((at + float(p * PACK) == code).astype(jnp.float32).astype(jnp.bfloat16))
    left = jnp.concatenate(left, axis=1)
    copies = []
    for c in range(made_ref.shape[0]):
        width = made_ref.shape[2]
        cols = slice(c * width, (c + 1) * width)
        right = jnp.concatenate([ref[:, cols] for ref in blocks], axis=0)
        made_ref[c] = jnp.dot(left, right, preferred_element_type=jnp.float32).astype(jnp.bfloat16)
        copy = pltpu.make_async_copy(made_ref.at[c], out_ref.at[:, cols], sems.at[c])
        copy.start()
        copies.append(copy)
    for copy in copies:
        copy.wait()


def pick_rows(plan, blocks):
    total, width = plan[0].shape[0], 512
    return pl.pallas_call(
        pick_kernel,
        out_shape=jax.ShapeDtypeStruct((total, D), jnp.bfloat16),
        out_specs=pl.BlockSpec(memory_space=pltpu.HBM),
        scratch_shapes=[
            pltpu.VMEM((D // width, total, width), jnp.bfloat16),
            pltpu.SemaphoreType.DMA((D // width,)),
        ],
        compiler_params=pltpu.CompilerParams(vmem_limit_bytes=24 * MIB),
        name="pick_rows",
    )(*plan, *blocks)


def unpick_places(distances, rows, offset, ring):
    out = jnp.arange(2 * ring * CAP, dtype=jnp.int32)
    distance = ((out // CAP) % ring - lax.axis_index("z")) % ring
    inside, listed = jnp.zeros(out.shape, bool), jnp.zeros_like(out)
    for i, d in enumerate(distances):
        here = distance == d % ring
        inside, listed = inside | here, jnp.where(here, i, listed)
    at = (out // (ring * CAP)) * rows + offset + listed * CAP + out % CAP
    return jnp.where(inside, at, -1)


def pack_matrix():
    side = PACK * CHUNKS
    a = lax.broadcasted_iota(jnp.int32, (side, side), 1)
    b = lax.broadcasted_iota(jnp.int32, (side, side), 0)
    return (b == (a % PACK) * CHUNKS + a // PACK).astype(jnp.float32).astype(jnp.bfloat16)


def expert_kernel(*refs):
    groups = len(DISTANCES)
    received, order_ref = refs[:groups], refs[groups]
    gate_ref, up_ref, down_ref, out_ref, x_ref, acc_ref = refs[groups + 1 :]
    part = pl.program_id(0)
    parts = pl.num_programs(0)
    side = PACK * CHUNKS
    blocks = out_ref.shape[0] // side

    @pl.when(part == 0)
    def _():
        rows = order_ref.shape[0]
        repeats = x_ref.shape[0] // rows
        orders = []
        for g, ref in enumerate(received):
            col = lax.broadcasted_iota(jnp.int32, (rows, ref.shape[0] // repeats), 1)
            same = order_ref[:, g : g + 1] == col
            orders.append(same.astype(jnp.float32).astype(jnp.bfloat16))
        for i in range(repeats):
            got = 0.0
            for ref, order in zip(received, orders):
                cols = order.shape[1]
                got = got + jnp.dot(
                    order,
                    ref[i * cols : (i + 1) * cols, :],
                    preferred_element_type=jnp.float32,
                )
            x_ref[i * rows : (i + 1) * rows, :] = got.astype(jnp.bfloat16)

    x = x_ref[...]
    joined = lambda ref: jnp.concatenate([ref[i, 0] for i in range(ref.shape[0])], axis=1)
    gate = jnp.dot(x, joined(gate_ref), preferred_element_type=jnp.float32)
    up = jnp.dot(x, joined(up_ref), preferred_element_type=jnp.float32)
    inner = (gate / (1.0 + jnp.exp(-gate)) * up).astype(jnp.bfloat16)
    out = lax.dot_general(
        inner, joined(down_ref), (((1,), (1,)), ((), ())), preferred_element_type=jnp.float32
    )

    @pl.when(part == 0)
    def _():
        acc_ref[...] = out

    @pl.when((part > 0) & (part < parts - 1))
    def _():
        acc_ref[...] += out

    @pl.when(part == parts - 1)
    def _():
        x_ref[...] = (acc_ref[...] + out).astype(jnp.bfloat16)
        pack = pack_matrix()
        for b in range(blocks):
            pieces = [
                x_ref[b * PACK : (b + 1) * PACK, j * WIDTH : (j + 1) * WIDTH]
                for j in range(CHUNKS)
            ]
            out_ref[b * side : (b + 1) * side, :] = jnp.dot(
                pack, jnp.concatenate(pieces, axis=0), preferred_element_type=jnp.float32
            ).astype(jnp.bfloat16)


def run_expert(received, order, weights, items):
    total = items * CHUNKS
    shares, _, _, width = weights.shape
    step = FF_BLOCK // width
    once = lambda a: pl.BlockSpec(a.shape, lambda f: (0, 0), pipeline_mode=pl.Buffered(1))
    return pl.pallas_call(
        expert_kernel,
        out_shape=jax.ShapeDtypeStruct((total, WIDTH), jnp.bfloat16),
        grid=(shares // step,),
        in_specs=[
            *(once(a) for a in (*received, order)),
            pl.BlockSpec((step, 1, D, width), lambda f: (f, 0, 0, 0)),
            pl.BlockSpec((step, 1, D, width), lambda f: (f, 1, 0, 0)),
            pl.BlockSpec((step, 1, D, width), lambda f: (f, 2, 0, 0)),
        ],
        out_specs=pl.BlockSpec((total, WIDTH), lambda f: (0, 0), pipeline_mode=pl.Buffered(1)),
        scratch_shapes=[
            pltpu.VMEM((items, D), jnp.bfloat16),
            pltpu.VMEM((items, D), jnp.float32),
        ],
        compiler_params=pltpu.CompilerParams(vmem_limit_bytes=54 * MIB),
        name="run_expert",
    )(*received, order, weights, weights, weights)


def combine_kernel(combine_ref, rows_ref, base_ref, out_ref):
    combine = combine_ref[...]
    which = lax.broadcasted_iota(jnp.int32, combine.shape, 1) % CHUNKS
    left = jnp.concatenate(
        [jnp.where(which == j, combine, jnp.zeros_like(combine)) for j in range(CHUNKS)], axis=0
    )
    got = jnp.dot(left, rows_ref[...], preferred_element_type=jnp.float32)
    tokens = combine.shape[0]
    for j in range(CHUNKS):
        cols = slice(j * WIDTH, (j + 1) * WIDTH)
        out_ref[:, cols] = (
            base_ref[:, cols].astype(jnp.float32) + got[j * tokens : (j + 1) * tokens, :]
        ).astype(out_ref.dtype)


def combine_rows(combine, rows, base, dtype):
    vmem = pl.BlockSpec(memory_space=pltpu.VMEM)
    return pl.pallas_call(
        combine_kernel,
        out_shape=jax.ShapeDtypeStruct(base.shape, dtype),
        in_specs=[vmem] * 3,
        out_specs=vmem,
        compiler_params=pltpu.CompilerParams(vmem_limit_bytes=32 * MIB),
        name="combine_rows",
    )(combine, rows, base)


def body(
    hidden,
    queries,
    latent,
    group_order,
    w_uk,
    w_uv,
    w_out,
    norm_gain,
    expert_ids,
    gate_weights,
    w_gate,
    w_up,
    w_down,
):
    ring, columns = lax.axis_size("z"), lax.axis_size("x")
    peers = columns * ring
    block_rows = hidden.shape[1]
    half_rows = block_rows // 2
    whole, places, query_rows = gather_latent(latent[0], queries[0].T)
    shares = (w_gate, w_up, w_down)
    weights = [gather_weights(shares, k) for k in range(LOCAL)]
    seq_rows = whole.shape[0]
    inside = jnp.arange(half_rows, dtype=jnp.int32)

    def positions_of(blocks):
        halves = (blocks[:, None] * 2 + jnp.arange(2, dtype=jnp.int32)[None, :]).reshape(-1)
        return (group_order[halves][:, None] * half_rows + inside[None, :]).reshape(-1)

    positions = positions_of(places)
    own_positions = positions_of(places[:1])
    rank_of, gate_of = routing(expert_ids[0], gate_weights[0])
    combines = [combine_weights(rank_of, gate_of, k, peers) for k in range(LOCAL)]
    both, alone = range(LOCAL), [[k] for k in range(LOCAL)]
    plans, orders = [], [[] for _ in both]
    for distances in DISTANCES:
        count = len(distances)
        together = distances is not DISTANCES[-1]
        plans.append([pick_plan(count, g, ring, columns) for g in ([both] if together else alone)])
        rows = group_rows(count * (LOCAL if together else 1))
        for k in both:
            offset = k * count * CAP if together else 0
            orders[k].append(unpick_places(distances, rows, offset, ring))
    orders = [jnp.stack(places_of, axis=1) for places_of in orders]
    table = jnp.pad(rank_of, ((0, 0), (0, EXTRA - EXPERTS)))
    content = whole[:, :KVR]
    key_rope = whole[:, KVR:]
    key_nope = jnp.dot(content, w_uk, preferred_element_type=jnp.float32).astype(jnp.bfloat16)
    values = jnp.dot(content, w_uv, preferred_element_type=jnp.float32).astype(jnp.bfloat16)
    query_full = query_rows.reshape(HEADS, NOPE + ROPE, block_rows)
    scores = jnp.einsum(
        "hdq,khd->hqk",
        query_full[:, :NOPE],
        key_nope.reshape(seq_rows, HEADS, NOPE),
        preferred_element_type=jnp.float32,
    )
    scores = scores + jnp.einsum(
        "hrq,kr->hqk", query_full[:, NOPE:], key_rope, preferred_element_type=jnp.float32
    )
    scores = scores * (NOPE + ROPE) ** (-0.5)
    visible = positions[None, :] <= own_positions[:, None]
    scores = jnp.where(visible[None], scores, -jnp.inf)
    peak = jnp.max(scores, axis=2, keepdims=True)
    expo = jnp.exp(scores - peak)
    totals = jnp.sum(expo, axis=2)
    heads_out = jnp.einsum(
        "hqk,khv->qhv",
        expo.astype(jnp.bfloat16),
        values.reshape(seq_rows, HEADS, VDIM),
        preferred_element_type=jnp.float32,
    )
    heads_out = heads_out / jnp.transpose(totals)[:, :, None]
    attended = heads_out.astype(jnp.bfloat16).reshape(block_rows, HEADS * VDIM)
    residual = (
        hidden[0].astype(jnp.float32) + jnp.dot(attended, w_out, preferred_element_type=jnp.float32)
    ).astype(jnp.bfloat16)
    stream = residual.astype(jnp.float32)
    factor = lax.rsqrt(jnp.mean(stream * stream, axis=1, keepdims=True) + EPSILON)
    normed = (stream * factor * norm_gain).astype(jnp.bfloat16)

    own = jnp.concatenate([normed, table], axis=1)
    def along_x(picked):
        picked = picked.reshape(columns, -1, D)
        return lax.all_to_all(picked, "x", split_axis=0, concat_axis=0, tiled=True).reshape(-1, D)

    up1, down1 = shifted(own, "z", 1), shifted(own, "z", -1)
    up2, down2 = shifted(up1, "z", 1), shifted(down1, "z", -1)
    first = pick_rows(plans[0][0], [up1, own, down1])
    from_first = along_x(first)
    second = pick_rows(plans[1][0], [up2, down2])
    _, up2, down2 = held(first, up2, down2)
    up3, down3 = shifted(up2, "z", 1), shifted(down2, "z", -1)
    second, _, orders = held(second, from_first, orders)
    from_second = along_x(second)
    half = block_rows // 2
    across = jnp.concatenate(
        [shifted(up3[:half], "z", 1), shifted(down3[half:], "z", -1)], axis=0
    )
    before, from_last = from_second, []
    for k in range(LOCAL):
        picked = pick_rows(plans[2][k], [down3, across, up3])
        picked, _ = held(picked, before)
        before = along_x(picked)
        from_last.append(before)
    items = peers * CAP
    returned = [
        exchanged(
            run_expert((from_first, from_second, from_last[k]), orders[k], weights[k], items),
            peers,
        )
        for k in range(LOCAL)
    ]
    mixed = residual
    for k in range(LOCAL):
        last = k == LOCAL - 1
        mixed = combine_rows(combines[k], returned[k], mixed, jnp.bfloat16 if last else jnp.float32)
    return mixed[None]


def solution(mesh):
    ctx, exp = mesh.devices.shape
    cores, ring = 2, 8
    mesh = Mesh(
        mesh.devices.reshape(ctx // cores, cores, exp // ring, ring), ("y", "core", "x", "z")
    )
    ctx, exp = ("y", "core"), ("x", "z")
    part, units = P(exp, ctx, None), P(exp, None, ctx)
    return jax.shard_map(
        body,
        mesh=mesh,
        in_specs=(part, part, part, P(), P(), P(), P(), P(), part, part, units, units, units),
        out_specs=part,
        check_vma=False,
    )
```

```python
import jax
import jax.numpy as jnp
from jax import lax
from jax.experimental import pallas as pl
from jax.experimental.pallas import tpu as pltpu
from jax.sharding import Mesh
from jax.sharding import PartitionSpec as P

D = 2048
HEADS = 8
NOPE = 128
ROPE = 64
VDIM = 128
KVR = 512
EXPERTS = 64
TOPK = 6
CAP = 13
EPSILON = 1e-06

CHUNKS = 8
WIDTH = D // CHUNKS
LOCAL = 2
BLOCK = CAP * CHUNKS
PACK = 16
FF_BLOCK = 256
MIB = 1 << 20

EXTRA = 128
DISTANCES = ((-1, 0, 1), (-2, 2), (3, 4, -3))


def gather_latent(own, ready):
    near = [own, shifted(own, "y", 1), shifted(own, "y", -1), shifted(own, "y", 2)]
    mine, ready = held(jnp.concatenate(near, axis=0), ready)
    whole = jnp.concatenate([mine, shifted(mine, "core", 1)], axis=0)
    length, cores = lax.axis_size("y"), lax.axis_size("core")
    along = (lax.axis_index("y") + jnp.array([0, -1, 1, -2], jnp.int32)) % length
    core = lax.axis_index("core")
    places = [along * cores + (core + i) % cores for i in range(cores)]
    return whole, jnp.concatenate(places), ready


def pack_kernel(*refs):
    shares, packed, sems = refs[:3], refs[3:-1], refs[-1]
    copies = [
        pltpu.make_async_copy(share.at[k], packed[k].at[i], sems.at[k, i])
        for k in range(len(packed))
        for i, share in enumerate(shares)
    ]
    for copy in copies:
        copy.start()
    for copy in copies:
        copy.wait()


def pack_weights(shares):
    hbm = pl.BlockSpec(memory_space=pltpu.HBM)
    one = jax.ShapeDtypeStruct((len(shares), *shares[0].shape[1:]), shares[0].dtype)
    return pl.pallas_call(
        pack_kernel,
        out_shape=[one] * LOCAL,
        in_specs=[hbm] * len(shares),
        out_specs=[hbm] * LOCAL,
        scratch_shapes=[pltpu.SemaphoreType.DMA((LOCAL, len(shares)))],
        name="pack_weights",
    )(*shares)


def exchanged(rows, peers):
    return lax.all_to_all(
        rows.reshape(peers, BLOCK, WIDTH), ("x", "z"), split_axis=0, concat_axis=0, tiled=True
    ).reshape(peers * BLOCK, WIDTH)


def routing(ids, gates):
    rows = ids.shape[0]
    chosen = ids[:, :, None] == jnp.arange(EXPERTS, dtype=jnp.int32)[None, None, :]
    named = jnp.any(chosen, axis=1)
    gate_of = jnp.sum(jnp.where(chosen, gates[:, :, None], 0.0), axis=1)
    order = jnp.arange(rows, dtype=jnp.int32)
    earlier = (order[None, :] < order[:, None]).astype(jnp.bfloat16)
    before = jnp.dot(earlier, named.astype(jnp.bfloat16), preferred_element_type=jnp.float32)
    rank_of = jnp.where(named, before, -1.0).astype(jnp.bfloat16)
    return rank_of, gate_of


def combine_weights(rank_of, gate_of, local, peers):
    total = peers * BLOCK
    row = jnp.arange(total, dtype=jnp.int32)
    expert = (row // BLOCK) * LOCAL + local
    rank = ((row % BLOCK) // CHUNKS).astype(jnp.float32)
    onehot = (expert[:, None] == jnp.arange(EXPERTS, dtype=jnp.int32)[None, :]).astype(jnp.bfloat16)
    at_cols = lax.dot_general(
        rank_of, onehot, (((1,), (1,)), ((), ())), preferred_element_type=jnp.float32
    )
    gate_cols = lax.dot_general(
        gate_of.astype(jnp.bfloat16),
        onehot,
        (((1,), (1,)), ((), ())),
        preferred_element_type=jnp.float32,
    )
    return jnp.where(at_cols == rank[None, :], gate_cols, 0.0).astype(jnp.bfloat16)


def shifted(rows, axis, by):
    length = lax.axis_size(axis)
    return lax.ppermute(rows, axis, [(i, (i + by) % length) for i in range(length)])


def held(*arrays):
    return lax.optimization_barrier(arrays)


def group_rows(count):
    return -(-count * CAP // 8) * 8


def pick_plan(count, locals_, ring, columns):
    rows = group_rows(count * len(locals_))
    row = jnp.arange(rows, dtype=jnp.int32)
    local = row // (count * CAP)
    block = (row // CAP) % count
    rank = row % CAP
    target = jnp.arange(columns, dtype=jnp.int32)
    first = (target * ring + lax.axis_index("z")) * LOCAL + locals_[0]
    expert = (first[:, None] + local[None, :]).reshape(-1)
    onehot = expert[:, None] == jnp.arange(EXTRA, dtype=jnp.int32)[None, :]
    code = jnp.where(local < len(locals_), block * PACK + rank, -PACK).astype(jnp.float32)
    code = jnp.broadcast_to(jnp.tile(code, columns)[:, None], (columns * rows, EXTRA))
    return onehot.astype(jnp.bfloat16), code


def pick_kernel(onehot_ref, code_ref, *refs):
    blocks, (out_ref, made_ref, sems) = refs[:-3], refs[-3:]
    onehot, code = onehot_ref[...], code_ref[...]
    left = []
    for p, ref in enumerate(blocks):
        at = lax.dot_general(
            onehot, ref[:, D:], (((1,), (1,)), ((), ())), preferred_element_type=jnp.float32
        )
        left.append((at + float(p * PACK) == code).astype(jnp.float32).astype(jnp.bfloat16))
    left = jnp.concatenate(left, axis=1)
    copies = []
    for c in range(made_ref.shape[0]):
        width = made_ref.shape[2]
        cols = slice(c * width, (c + 1) * width)
        right = jnp.concatenate([ref[:, cols] for ref in blocks], axis=0)
        made_ref[c] = jnp.dot(left, right, preferred_element_type=jnp.float32).astype(jnp.bfloat16)
        copy = pltpu.make_async_copy(made_ref.at[c], out_ref.at[:, cols], sems.at[c])
        copy.start()
        copies.append(copy)
    for copy in copies:
        copy.wait()


def pick_rows(plan, blocks):
    total, width = plan[0].shape[0], 512
    return pl.pallas_call(
        pick_kernel,
        out_shape=jax.ShapeDtypeStruct((total, D), jnp.bfloat16),
        out_specs=pl.BlockSpec(memory_space=pltpu.HBM),
        scratch_shapes=[
            pltpu.VMEM((D // width, total, width), jnp.bfloat16),
            pltpu.SemaphoreType.DMA((D // width,)),
        ],
        compiler_params=pltpu.CompilerParams(vmem_limit_bytes=24 * MIB),
        name="pick_rows",
    )(*plan, *blocks)


def unpick_places(distances, rows, offset, ring):
    out = jnp.arange(2 * ring * CAP, dtype=jnp.int32)
    distance = ((out // CAP) % ring - lax.axis_index("z")) % ring
    inside, listed = jnp.zeros(out.shape, bool), jnp.zeros_like(out)
    for i, d in enumerate(distances):
        here = distance == d % ring
        inside, listed = inside | here, jnp.where(here, i, listed)
    at = (out // (ring * CAP)) * rows + offset + listed * CAP + out % CAP
    return jnp.where(inside, at, -1)


def pack_matrix():
    side = PACK * CHUNKS
    a = lax.broadcasted_iota(jnp.int32, (side, side), 1)
    b = lax.broadcasted_iota(jnp.int32, (side, side), 0)
    return (b == (a % PACK) * CHUNKS + a // PACK).astype(jnp.float32).astype(jnp.bfloat16)


def expert_kernel(*refs):
    groups = len(DISTANCES)
    received, order_ref = refs[:groups], refs[groups]
    gate_ref, up_ref, down_ref, out_ref, x_ref, acc_ref = refs[groups + 1 :]
    part = pl.program_id(0)
    parts = pl.num_programs(0)
    side = PACK * CHUNKS
    blocks = out_ref.shape[0] // side

    @pl.when(part == 0)
    def _():
        rows = order_ref.shape[0]
        repeats = x_ref.shape[0] // rows
        orders = []
        for g, ref in enumerate(received):
            col = lax.broadcasted_iota(jnp.int32, (rows, ref.shape[0] // repeats), 1)
            same = order_ref[:, g : g + 1] == col
            orders.append(same.astype(jnp.float32).astype(jnp.bfloat16))
        for i in range(repeats):
            got = 0.0
            for ref, order in zip(received, orders):
                cols = order.shape[1]
                got = got + jnp.dot(
                    order,
                    ref[i * cols : (i + 1) * cols, :],
                    preferred_element_type=jnp.float32,
                )
            x_ref[i * rows : (i + 1) * rows, :] = got.astype(jnp.bfloat16)

    x = x_ref[...]
    joined = lambda ref: jnp.concatenate([ref[i, 0] for i in range(ref.shape[0])], axis=1)
    gate = jnp.dot(x, joined(gate_ref), preferred_element_type=jnp.float32)
    up = jnp.dot(x, joined(up_ref), preferred_element_type=jnp.float32)
    inner = (gate / (1.0 + jnp.exp(-gate)) * up).astype(jnp.bfloat16)
    out = lax.dot_general(
        inner, joined(down_ref), (((1,), (1,)), ((), ())), preferred_element_type=jnp.float32
    )

    @pl.when(part == 0)
    def _():
        acc_ref[...] = out

    @pl.when((part > 0) & (part < parts - 1))
    def _():
        acc_ref[...] += out

    @pl.when(part == parts - 1)
    def _():
        x_ref[...] = (acc_ref[...] + out).astype(jnp.bfloat16)
        pack = pack_matrix()
        for b in range(blocks):
            pieces = [
                x_ref[b * PACK : (b + 1) * PACK, j * WIDTH : (j + 1) * WIDTH]
                for j in range(CHUNKS)
            ]
            out_ref[b * side : (b + 1) * side, :] = jnp.dot(
                pack, jnp.concatenate(pieces, axis=0), preferred_element_type=jnp.float32
            ).astype(jnp.bfloat16)


def run_expert(received, order, weights, items):
    total = items * CHUNKS
    shares, _, _, width = weights.shape
    step = FF_BLOCK // width
    once = lambda a: pl.BlockSpec(a.shape, lambda f: (0, 0), pipeline_mode=pl.Buffered(1))
    return pl.pallas_call(
        expert_kernel,
        out_shape=jax.ShapeDtypeStruct((total, WIDTH), jnp.bfloat16),
        grid=(shares // step,),
        in_specs=[
            *(once(a) for a in (*received, order)),
            pl.BlockSpec((step, 1, D, width), lambda f: (f, 0, 0, 0)),
            pl.BlockSpec((step, 1, D, width), lambda f: (f, 1, 0, 0)),
            pl.BlockSpec((step, 1, D, width), lambda f: (f, 2, 0, 0)),
        ],
        out_specs=pl.BlockSpec((total, WIDTH), lambda f: (0, 0), pipeline_mode=pl.Buffered(1)),
        scratch_shapes=[
            pltpu.VMEM((items, D), jnp.bfloat16),
            pltpu.VMEM((items, D), jnp.float32),
        ],
        compiler_params=pltpu.CompilerParams(vmem_limit_bytes=54 * MIB),
        name="run_expert",
    )(*received, order, weights, weights, weights)


def combine_kernel(combine_ref, rows_ref, base_ref, out_ref):
    combine = combine_ref[...]
    which = lax.broadcasted_iota(jnp.int32, combine.shape, 1) % CHUNKS
    left = jnp.concatenate(
        [jnp.where(which == j, combine, jnp.zeros_like(combine)) for j in range(CHUNKS)], axis=0
    )
    got = jnp.dot(left, rows_ref[...], preferred_element_type=jnp.float32)
    tokens = combine.shape[0]
    for j in range(CHUNKS):
        cols = slice(j * WIDTH, (j + 1) * WIDTH)
        out_ref[:, cols] = (
            base_ref[:, cols].astype(jnp.float32) + got[j * tokens : (j + 1) * tokens, :]
        ).astype(out_ref.dtype)


def combine_rows(combine, rows, base, dtype):
    vmem = pl.BlockSpec(memory_space=pltpu.VMEM)
    return pl.pallas_call(
        combine_kernel,
        out_shape=jax.ShapeDtypeStruct(base.shape, dtype),
        in_specs=[vmem] * 3,
        out_specs=vmem,
        compiler_params=pltpu.CompilerParams(vmem_limit_bytes=32 * MIB),
        name="combine_rows",
    )(combine, rows, base)


def body(
    hidden,
    queries,
    latent,
    group_order,
    w_uk,
    w_uv,
    w_out,
    norm_gain,
    expert_ids,
    gate_weights,
    w_gate,
    w_up,
    w_down,
):
    ring, columns = lax.axis_size("z"), lax.axis_size("x")
    peers = columns * ring
    block_rows = hidden.shape[1]
    half_rows = block_rows // 2
    whole, places, query_rows = gather_latent(latent[0], queries[0].T)
    packed = pack_weights((w_gate, w_up, w_down))
    weights = [lax.all_gather(one, ("y", "core"), axis=0) for one in packed]
    seq_rows = whole.shape[0]
    inside = jnp.arange(half_rows, dtype=jnp.int32)

    def positions_of(blocks):
        halves = (blocks[:, None] * 2 + jnp.arange(2, dtype=jnp.int32)[None, :]).reshape(-1)
        return (group_order[halves][:, None] * half_rows + inside[None, :]).reshape(-1)

    positions = positions_of(places)
    own_positions = positions_of(places[:1])
    rank_of, gate_of = routing(expert_ids[0], gate_weights[0])
    combines = [combine_weights(rank_of, gate_of, k, peers) for k in range(LOCAL)]
    both, alone = range(LOCAL), [[k] for k in range(LOCAL)]
    plans, orders = [], [[] for _ in both]
    for distances in DISTANCES:
        count = len(distances)
        together = distances is not DISTANCES[-1]
        plans.append([pick_plan(count, g, ring, columns) for g in ([both] if together else alone)])
        rows = group_rows(count * (LOCAL if together else 1))
        for k in both:
            offset = k * count * CAP if together else 0
            orders[k].append(unpick_places(distances, rows, offset, ring))
    orders = [jnp.stack(places_of, axis=1) for places_of in orders]
    table = jnp.pad(rank_of, ((0, 0), (0, EXTRA - EXPERTS)))
    content = whole[:, :KVR]
    key_rope = whole[:, KVR:]
    key_nope = jnp.dot(content, w_uk, preferred_element_type=jnp.float32).astype(jnp.bfloat16)
    values = jnp.dot(content, w_uv, preferred_element_type=jnp.float32).astype(jnp.bfloat16)
    query_full = query_rows.reshape(HEADS, NOPE + ROPE, block_rows)
    scores = jnp.einsum(
        "hdq,khd->hqk",
        query_full[:, :NOPE],
        key_nope.reshape(seq_rows, HEADS, NOPE),
        preferred_element_type=jnp.float32,
    )
    scores = scores + jnp.einsum(
        "hrq,kr->hqk", query_full[:, NOPE:], key_rope, preferred_element_type=jnp.float32
    )
    scores = scores * (NOPE + ROPE) ** (-0.5)
    visible = positions[None, :] <= own_positions[:, None]
    scores = jnp.where(visible[None], scores, -jnp.inf)
    peak = jnp.max(scores, axis=2, keepdims=True)
    expo = jnp.exp(scores - peak)
    totals = jnp.sum(expo, axis=2)
    heads_out = jnp.einsum(
        "hqk,khv->qhv",
        expo.astype(jnp.bfloat16),
        values.reshape(seq_rows, HEADS, VDIM),
        preferred_element_type=jnp.float32,
    )
    heads_out = heads_out / jnp.transpose(totals)[:, :, None]
    attended = heads_out.astype(jnp.bfloat16).reshape(block_rows, HEADS * VDIM)
    residual = (
        hidden[0].astype(jnp.float32) + jnp.dot(attended, w_out, preferred_element_type=jnp.float32)
    ).astype(jnp.bfloat16)
    stream = residual.astype(jnp.float32)
    factor = lax.rsqrt(jnp.mean(stream * stream, axis=1, keepdims=True) + EPSILON)
    normed = (stream * factor * norm_gain).astype(jnp.bfloat16)

    own = jnp.concatenate([normed, table], axis=1)
    def along_x(picked):
        picked = picked.reshape(columns, -1, D)
        return lax.all_to_all(picked, "x", split_axis=0, concat_axis=0, tiled=True).reshape(-1, D)

    up1, down1 = shifted(own, "z", 1), shifted(own, "z", -1)
    up2, down2 = shifted(up1, "z", 1), shifted(down1, "z", -1)
    first = pick_rows(plans[0][0], [up1, own, down1])
    from_first = along_x(first)
    second = pick_rows(plans[1][0], [up2, down2])
    _, up2, down2 = held(first, up2, down2)
    up3, down3 = shifted(up2, "z", 1), shifted(down2, "z", -1)
    second, _, orders = held(second, from_first, orders)
    from_second = along_x(second)
    half = block_rows // 2
    across = jnp.concatenate(
        [shifted(up3[:half], "z", 1), shifted(down3[half:], "z", -1)], axis=0
    )
    before, from_last = from_second, []
    for k in range(LOCAL):
        picked = pick_rows(plans[2][k], [down3, across, up3])
        picked, _ = held(picked, before)
        before = along_x(picked)
        from_last.append(before)
    items = peers * CAP
    returned = [
        exchanged(
            run_expert((from_first, from_second, from_last[k]), orders[k], weights[k], items),
            peers,
        )
        for k in range(LOCAL)
    ]
    mixed = residual
    for k in range(LOCAL):
        last = k == LOCAL - 1
        mixed = combine_rows(combines[k], returned[k], mixed, jnp.bfloat16 if last else jnp.float32)
    return mixed[None]


def solution(mesh):
    ctx, exp = mesh.devices.shape
    cores, ring = 2, 8
    mesh = Mesh(
        mesh.devices.reshape(ctx // cores, cores, exp // ring, ring), ("y", "core", "x", "z")
    )
    ctx, exp = ("y", "core"), ("x", "z")
    part, units = P(exp, ctx, None), P(exp, None, ctx)
    return jax.shard_map(
        body,
        mesh=mesh,
        in_specs=(part, part, part, P(), P(), P(), P(), P(), part, part, units, units, units),
        out_specs=part,
        check_vma=False,
    )
```

```python
import jax
import jax.numpy as jnp
from jax import lax
from jax.experimental import pallas as pl
from jax.experimental.pallas import tpu as pltpu
from jax.sharding import Mesh
from jax.sharding import PartitionSpec as P

D = 2048
HEADS = 8
NOPE = 128
ROPE = 64
VDIM = 128
KVR = 512
EXPERTS = 64
TOPK = 6
CAP = 13
EPSILON = 1e-06

CHUNKS = 8
WIDTH = D // CHUNKS
LOCAL = 2
BLOCK = CAP * CHUNKS
PACK = 16
FF_BLOCK = 512
MIB = 1 << 20

EXTRA = 128
DISTANCES = ((-1, 0, 1), (-2, 2), (3, 4, -3))


def gather_latent(own, ready):
    near = [own, shifted(own, "y", 1), shifted(own, "y", -1), shifted(own, "y", 2)]
    mine, ready = held(jnp.concatenate(near, axis=0), ready)
    whole = jnp.concatenate([mine, shifted(mine, "core", 1)], axis=0)
    length, cores = lax.axis_size("y"), lax.axis_size("core")
    along = (lax.axis_index("y") + jnp.array([0, -1, 1, -2], jnp.int32)) % length
    core = lax.axis_index("core")
    places = [along * cores + (core + i) % cores for i in range(cores)]
    return whole, jnp.concatenate(places), ready


def gather_weights(shares, local):
    stack = jnp.concatenate([w[local : local + 1] for w in shares])
    return lax.all_gather(stack, ("y", "core"), axis=0)


def exchanged(rows, peers):
    return lax.all_to_all(
        rows.reshape(peers, BLOCK, WIDTH), ("x", "z"), split_axis=0, concat_axis=0, tiled=True
    ).reshape(peers * BLOCK, WIDTH)


def routing(ids, gates):
    rows = ids.shape[0]
    chosen = ids[:, :, None] == jnp.arange(EXPERTS, dtype=jnp.int32)[None, None, :]
    named = jnp.any(chosen, axis=1)
    gate_of = jnp.sum(jnp.where(chosen, gates[:, :, None], 0.0), axis=1)
    order = jnp.arange(rows, dtype=jnp.int32)
    earlier = (order[None, :] < order[:, None]).astype(jnp.bfloat16)
    before = jnp.dot(earlier, named.astype(jnp.bfloat16), preferred_element_type=jnp.float32)
    rank_of = jnp.where(named, before, -1.0).astype(jnp.bfloat16)
    return rank_of, gate_of


def combine_weights(rank_of, gate_of, local, peers):
    total = peers * BLOCK
    row = jnp.arange(total, dtype=jnp.int32)
    expert = (row // BLOCK) * LOCAL + local
    rank = ((row % BLOCK) // CHUNKS).astype(jnp.float32)
    onehot = (expert[:, None] == jnp.arange(EXPERTS, dtype=jnp.int32)[None, :]).astype(jnp.bfloat16)
    at_cols = lax.dot_general(
        rank_of, onehot, (((1,), (1,)), ((), ())), preferred_element_type=jnp.float32
    )
    gate_cols = lax.dot_general(
        gate_of.astype(jnp.bfloat16),
        onehot,
        (((1,), (1,)), ((), ())),
        preferred_element_type=jnp.float32,
    )
    return jnp.where(at_cols == rank[None, :], gate_cols, 0.0).astype(jnp.bfloat16)


def shifted(rows, axis, by):
    length = lax.axis_size(axis)
    return lax.ppermute(rows, axis, [(i, (i + by) % length) for i in range(length)])


def held(*arrays):
    return lax.optimization_barrier(arrays)


def group_rows(count):
    return -(-count * CAP // 8) * 8


def pick_plan(count, locals_, ring, columns):
    rows = group_rows(count * len(locals_))
    row = jnp.arange(rows, dtype=jnp.int32)
    local = row // (count * CAP)
    block = (row // CAP) % count
    rank = row % CAP
    target = jnp.arange(columns, dtype=jnp.int32)
    first = (target * ring + lax.axis_index("z")) * LOCAL + locals_[0]
    expert = (first[:, None] + local[None, :]).reshape(-1)
    onehot = expert[:, None] == jnp.arange(EXTRA, dtype=jnp.int32)[None, :]
    code = jnp.where(local < len(locals_), block * PACK + rank, -PACK).astype(jnp.float32)
    code = jnp.broadcast_to(jnp.tile(code, columns)[:, None], (columns * rows, EXTRA))
    return onehot.astype(jnp.bfloat16), code


def pick_kernel(onehot_ref, code_ref, *refs):
    blocks, (out_ref, made_ref, sems) = refs[:-3], refs[-3:]
    onehot, code = onehot_ref[...], code_ref[...]
    left = []
    for p, ref in enumerate(blocks):
        at = lax.dot_general(
            onehot, ref[:, D:], (((1,), (1,)), ((), ())), preferred_element_type=jnp.float32
        )
        left.append((at + float(p * PACK) == code).astype(jnp.float32).astype(jnp.bfloat16))
    left = jnp.concatenate(left, axis=1)
    copies = []
    for c in range(made_ref.shape[0]):
        width = made_ref.shape[2]
        cols = slice(c * width, (c + 1) * width)
        right = jnp.concatenate([ref[:, cols] for ref in blocks], axis=0)
        made_ref[c] = jnp.dot(left, right, preferred_element_type=jnp.float32).astype(jnp.bfloat16)
        copy = pltpu.make_async_copy(made_ref.at[c], out_ref.at[:, cols], sems.at[c])
        copy.start()
        copies.append(copy)
    for copy in copies:
        copy.wait()


def pick_rows(plan, blocks):
    total, width = plan[0].shape[0], 512
    return pl.pallas_call(
        pick_kernel,
        out_shape=jax.ShapeDtypeStruct((total, D), jnp.bfloat16),
        out_specs=pl.BlockSpec(memory_space=pltpu.HBM),
        scratch_shapes=[
            pltpu.VMEM((D // width, total, width), jnp.bfloat16),
            pltpu.SemaphoreType.DMA((D // width,)),
        ],
        compiler_params=pltpu.CompilerParams(vmem_limit_bytes=24 * MIB),
        name="pick_rows",
    )(*plan, *blocks)


def unpick_places(distances, rows, offset, ring):
    out = jnp.arange(2 * ring * CAP, dtype=jnp.int32)
    distance = ((out // CAP) % ring - lax.axis_index("z")) % ring
    inside, listed = jnp.zeros(out.shape, bool), jnp.zeros_like(out)
    for i, d in enumerate(distances):
        here = distance == d % ring
        inside, listed = inside | here, jnp.where(here, i, listed)
    at = (out // (ring * CAP)) * rows + offset + listed * CAP + out % CAP
    return jnp.where(inside, at, -1)


def pack_matrix():
    side = PACK * CHUNKS
    a = lax.broadcasted_iota(jnp.int32, (side, side), 1)
    b = lax.broadcasted_iota(jnp.int32, (side, side), 0)
    return (b == (a % PACK) * CHUNKS + a // PACK).astype(jnp.float32).astype(jnp.bfloat16)


def expert_kernel(*refs):
    groups = len(DISTANCES)
    received, order_ref = refs[:groups], refs[groups]
    gate_ref, up_ref, down_ref, out_ref, x_ref, acc_ref = refs[groups + 1 :]
    part = pl.program_id(0)
    parts = pl.num_programs(0)
    side = PACK * CHUNKS
    blocks = out_ref.shape[0] // side

    @pl.when(part == 0)
    def _():
        rows = order_ref.shape[0]
        repeats = x_ref.shape[0] // rows
        orders = []
        for g, ref in enumerate(received):
            col = lax.broadcasted_iota(jnp.int32, (rows, ref.shape[0] // repeats), 1)
            same = order_ref[:, g : g + 1] == col
            orders.append(same.astype(jnp.float32).astype(jnp.bfloat16))
        for i in range(repeats):
            got = 0.0
            for ref, order in zip(received, orders):
                cols = order.shape[1]
                got = got + jnp.dot(
                    order,
                    ref[i * cols : (i + 1) * cols, :],
                    preferred_element_type=jnp.float32,
                )
            x_ref[i * rows : (i + 1) * rows, :] = got.astype(jnp.bfloat16)

    x = x_ref[...]
    joined = lambda ref: jnp.concatenate([ref[i, 0] for i in range(ref.shape[0])], axis=1)
    gate = jnp.dot(x, joined(gate_ref), preferred_element_type=jnp.float32)
    up = jnp.dot(x, joined(up_ref), preferred_element_type=jnp.float32)
    inner = (gate / (1.0 + jnp.exp(-gate)) * up).astype(jnp.bfloat16)
    out = lax.dot_general(
        inner, joined(down_ref), (((1,), (1,)), ((), ())), preferred_element_type=jnp.float32
    )

    @pl.when(part == 0)
    def _():
        acc_ref[...] = out

    @pl.when((part > 0) & (part < parts - 1))
    def _():
        acc_ref[...] += out

    @pl.when(part == parts - 1)
    def _():
        x_ref[...] = (acc_ref[...] + out).astype(jnp.bfloat16)
        pack = pack_matrix()
        for b in range(blocks):
            pieces = [
                x_ref[b * PACK : (b + 1) * PACK, j * WIDTH : (j + 1) * WIDTH]
                for j in range(CHUNKS)
            ]
            out_ref[b * side : (b + 1) * side, :] = jnp.dot(
                pack, jnp.concatenate(pieces, axis=0), preferred_element_type=jnp.float32
            ).astype(jnp.bfloat16)


def run_expert(received, order, weights, items):
    total = items * CHUNKS
    shares, _, _, width = weights.shape
    step = FF_BLOCK // width
    once = lambda a: pl.BlockSpec(a.shape, lambda f: (0, 0), pipeline_mode=pl.Buffered(1))
    return pl.pallas_call(
        expert_kernel,
        out_shape=jax.ShapeDtypeStruct((total, WIDTH), jnp.bfloat16),
        grid=(shares // step,),
        in_specs=[
            *(once(a) for a in (*received, order)),
            pl.BlockSpec((step, 1, D, width), lambda f: (f, 0, 0, 0)),
            pl.BlockSpec((step, 1, D, width), lambda f: (f, 1, 0, 0)),
            pl.BlockSpec((step, 1, D, width), lambda f: (f, 2, 0, 0)),
        ],
        out_specs=pl.BlockSpec((total, WIDTH), lambda f: (0, 0), pipeline_mode=pl.Buffered(1)),
        scratch_shapes=[
            pltpu.VMEM((items, D), jnp.bfloat16),
            pltpu.VMEM((items, D), jnp.float32),
        ],
        compiler_params=pltpu.CompilerParams(vmem_limit_bytes=54 * MIB),
        name="run_expert",
    )(*received, order, weights, weights, weights)


def combine_kernel(combine_ref, rows_ref, base_ref, out_ref):
    combine = combine_ref[...]
    which = lax.broadcasted_iota(jnp.int32, combine.shape, 1) % CHUNKS
    left = jnp.concatenate(
        [jnp.where(which == j, combine, jnp.zeros_like(combine)) for j in range(CHUNKS)], axis=0
    )
    got = jnp.dot(left, rows_ref[...], preferred_element_type=jnp.float32)
    tokens = combine.shape[0]
    for j in range(CHUNKS):
        cols = slice(j * WIDTH, (j + 1) * WIDTH)
        out_ref[:, cols] = (
            base_ref[:, cols].astype(jnp.float32) + got[j * tokens : (j + 1) * tokens, :]
        ).astype(out_ref.dtype)


def combine_rows(combine, rows, base, dtype):
    vmem = pl.BlockSpec(memory_space=pltpu.VMEM)
    return pl.pallas_call(
        combine_kernel,
        out_shape=jax.ShapeDtypeStruct(base.shape, dtype),
        in_specs=[vmem] * 3,
        out_specs=vmem,
        compiler_params=pltpu.CompilerParams(vmem_limit_bytes=32 * MIB),
        name="combine_rows",
    )(combine, rows, base)


def body(
    hidden,
    queries,
    latent,
    group_order,
    w_uk,
    w_uv,
    w_out,
    norm_gain,
    expert_ids,
    gate_weights,
    w_gate,
    w_up,
    w_down,
):
    ring, columns = lax.axis_size("z"), lax.axis_size("x")
    peers = columns * ring
    block_rows = hidden.shape[1]
    half_rows = block_rows // 2
    whole, places, query_rows = gather_latent(latent[0], queries[0].T)
    shares = (w_gate, w_up, w_down)
    weights = [gather_weights(shares, k) for k in range(LOCAL)]
    seq_rows = whole.shape[0]
    inside = jnp.arange(half_rows, dtype=jnp.int32)

    def positions_of(blocks):
        halves = (blocks[:, None] * 2 + jnp.arange(2, dtype=jnp.int32)[None, :]).reshape(-1)
        return (group_order[halves][:, None] * half_rows + inside[None, :]).reshape(-1)

    positions = positions_of(places)
    own_positions = positions_of(places[:1])
    rank_of, gate_of = routing(expert_ids[0], gate_weights[0])
    combines = [combine_weights(rank_of, gate_of, k, peers) for k in range(LOCAL)]
    both, alone = range(LOCAL), [[k] for k in range(LOCAL)]
    plans, orders = [], [[] for _ in both]
    for distances in DISTANCES:
        count = len(distances)
        together = distances is not DISTANCES[-1]
        plans.append([pick_plan(count, g, ring, columns) for g in ([both] if together else alone)])
        rows = group_rows(count * (LOCAL if together else 1))
        for k in both:
            offset = k * count * CAP if together else 0
            orders[k].append(unpick_places(distances, rows, offset, ring))
    orders = [jnp.stack(places_of, axis=1) for places_of in orders]
    table = jnp.pad(rank_of, ((0, 0), (0, EXTRA - EXPERTS)))
    content = whole[:, :KVR]
    key_rope = whole[:, KVR:]
    key_nope = jnp.dot(content, w_uk, preferred_element_type=jnp.float32).astype(jnp.bfloat16)
    values = jnp.dot(content, w_uv, preferred_element_type=jnp.float32).astype(jnp.bfloat16)
    query_full = query_rows.reshape(HEADS, NOPE + ROPE, block_rows)
    scores = jnp.einsum(
        "hdq,khd->hqk",
        query_full[:, :NOPE],
        key_nope.reshape(seq_rows, HEADS, NOPE),
        preferred_element_type=jnp.float32,
    )
    scores = scores + jnp.einsum(
        "hrq,kr->hqk", query_full[:, NOPE:], key_rope, preferred_element_type=jnp.float32
    )
    scores = scores * (NOPE + ROPE) ** (-0.5)
    visible = positions[None, :] <= own_positions[:, None]
    scores = jnp.where(visible[None], scores, -jnp.inf)
    peak = jnp.max(scores, axis=2, keepdims=True)
    expo = jnp.exp(scores - peak)
    totals = jnp.sum(expo, axis=2)
    heads_out = jnp.einsum(
        "hqk,khv->qhv",
        expo.astype(jnp.bfloat16),
        values.reshape(seq_rows, HEADS, VDIM),
        preferred_element_type=jnp.float32,
    )
    heads_out = heads_out / jnp.transpose(totals)[:, :, None]
    attended = heads_out.astype(jnp.bfloat16).reshape(block_rows, HEADS * VDIM)
    residual = (
        hidden[0].astype(jnp.float32) + jnp.dot(attended, w_out, preferred_element_type=jnp.float32)
    ).astype(jnp.bfloat16)
    stream = residual.astype(jnp.float32)
    factor = lax.rsqrt(jnp.mean(stream * stream, axis=1, keepdims=True) + EPSILON)
    normed = (stream * factor * norm_gain).astype(jnp.bfloat16)

    own = jnp.concatenate([normed, table], axis=1)
    def along_x(picked):
        picked = picked.reshape(columns, -1, D)
        return lax.all_to_all(picked, "x", split_axis=0, concat_axis=0, tiled=True).reshape(-1, D)

    up1, down1 = shifted(own, "z", 1), shifted(own, "z", -1)
    up2, down2 = shifted(up1, "z", 1), shifted(down1, "z", -1)
    first = pick_rows(plans[0][0], [up1, own, down1])
    from_first = along_x(first)
    second = pick_rows(plans[1][0], [up2, down2])
    _, up2, down2 = held(first, up2, down2)
    up3, down3 = shifted(up2, "z", 1), shifted(down2, "z", -1)
    second, _, orders = held(second, from_first, orders)
    from_second = along_x(second)
    half = block_rows // 2
    across = jnp.concatenate(
        [shifted(up3[:half], "z", 1), shifted(down3[half:], "z", -1)], axis=0
    )
    before, from_last = from_second, []
    for k in range(LOCAL):
        picked = pick_rows(plans[2][k], [down3, across, up3])
        picked, _ = held(picked, before)
        before = along_x(picked)
        from_last.append(before)
    items = peers * CAP
    returned = [
        exchanged(
            run_expert((from_first, from_second, from_last[k]), orders[k], weights[k], items),
            peers,
        )
        for k in range(LOCAL)
    ]
    mixed = residual
    for k in range(LOCAL):
        last = k == LOCAL - 1
        mixed = combine_rows(combines[k], returned[k], mixed, jnp.bfloat16 if last else jnp.float32)
    return mixed[None]


def solution(mesh):
    ctx, exp = mesh.devices.shape
    cores, ring = 2, 8
    mesh = Mesh(
        mesh.devices.reshape(ctx // cores, cores, exp // ring, ring), ("y", "core", "x", "z")
    )
    ctx, exp = ("y", "core"), ("x", "z")
    part, units = P(exp, ctx, None), P(exp, None, ctx)
    return jax.shard_map(
        body,
        mesh=mesh,
        in_specs=(part, part, part, P(), P(), P(), P(), P(), part, part, units, units, units),
        out_specs=part,
        check_vma=False,
    )
```
